32 devices in a mesh: step: 8 (over y, x, core), lat: 4 (over z).
Axes of the slice: x: 2, y: 2, z: 4, core: 2. Of those that a mesh axis runs over, the one named last changes fastest.
Arguments:
- state_in: bfloat16 [8, 72, 64, 128], P('step', None, 'lat'), may hold values from -6 to 6
- new_state: bfloat16 [72, 64, 128], P(None, 'lat'), may hold values from -6 to 6
- cot_early: bfloat16 [8, 72, 64, 128], P('step', None, 'lat'), may hold values from -6 to 6
- cot_late: bfloat16 [8, 72, 64, 128], P('step', None, 'lat'), may hold values from -6 to 6
- kernel_first: bfloat16 [9, 72, 192], replicated, may hold values from -0.25 to 0.25
- kernel_mid: bfloat16 [9, 192, 192], replicated, may hold values from -0.15625 to 0.15625
- kernel_last: bfloat16 [9, 72, 192], replicated, may hold values from -0.15625 to 0.15625
Outputs:
- advanced: bfloat16 [8, 72, 64, 128], P('step', None, 'lat')
- state_adjoint: bfloat16 [8, 72, 64, 128], P('step', None, 'lat')
- grad_first: float32 [9, 72, 192], replicated
- grad_mid: float32 [9, 192, 192], replicated
- grad_last: float32 [9, 72, 192], replicated
The draws below stay inside these ranges and needn't reach their ends.
All inputs are finite; a program needn't handle non-finite values.
Results may differ from the reference program's by a relative error of at most 0.008.
Values may be sent and summed in bfloat16 or wider, within the bound.
A program may use at most 64 MiB of HBM per device.

```python
import math
import jax
import jax.numpy as jnp
from jax import lax

CH = 72
HID = 192
COLS = 128
STEPS = 8
ROWS = 64


def levels(key, dims, pieces, smallest, high):
    gain = 1.0
    for axis_at, parts in pieces:
        heights = jax.random.uniform(jax.random.fold_in(jax.random.fold_in(key, 6), axis_at), (parts,), jnp.float32, smallest / len(pieces), high / len(pieces))
        gain = gain * jnp.repeat(jnp.exp(heights), dims[axis_at] // parts).reshape((-1,) + (1,) * (len(dims) - 1 - axis_at))
    return gain


def normal_values(own_key, dims, width, most, pieces=(), dtype=jnp.bfloat16):
    loudness = levels(own_key, dims, pieces, -0.22, 0.18) if pieces else 1.0
    entries = jax.random.normal(own_key, dims, jnp.float32) * width * loudness
    return jnp.minimum(jnp.maximum(entries, -most), most).astype(dtype)


def setup_inputs(seed: int = 0) -> dict:
    keys = jax.random.split(jax.random.key(seed), 8)
    return {
        "state_in": normal_values(keys[0], (STEPS, CH, ROWS, COLS), 1.0, 6.0, ((0, 8), (2, 4))),
        "new_state": normal_values(keys[1], (CH, ROWS, COLS), 1.0, 6.0, ((1, 4),)),
        "cot_early": normal_values(keys[2], (STEPS, CH, ROWS, COLS), 1.0, 6.0, ((0, 8), (2, 4))),
        "cot_late": normal_values(keys[3], (STEPS, CH, ROWS, COLS), 1.0, 6.0, ((0, 8), (2, 4))),
        "kernel_first": normal_values(keys[4], (9, CH, HID), (9 * CH) ** -0.5, 0.25),
        "kernel_mid": normal_values(keys[5], (9, HID, HID), (9 * HID) ** -0.5, 0.15625),
        "kernel_last": normal_values(keys[6], (9, CH, HID), (9 * HID) ** -0.5, 0.15625),
    }


def pad_rows(values, dilation):
    return jnp.pad(values, ((0, 0), (dilation, dilation), (0, 0)))

def window_at(padded, dilation, row_tap, col_tap, out_rows, out_cols):
    widened = jnp.pad(padded, ((0, 0), (0, 0), (dilation, dilation)))
    return widened[:, row_tap * dilation:row_tap * dilation + out_rows, col_tap * dilation:col_tap * dilation + out_cols]

def convolve(padded, kernel, dilation, flipped):
    out_rows = padded.shape[1] - 2 * dilation
    out_cols = padded.shape[2]
    pattern = 'oc,crw->orw' if flipped else 'co,crw->orw'
    summed = None
    for tap_index in range(9):
        window = window_at(padded, dilation, tap_index // 3, tap_index % 3, out_rows, out_cols)
        product = jnp.einsum(pattern, kernel[tap_index].astype(jnp.float32), window.astype(jnp.float32))
        summed = product if summed is None else summed + product
    return summed

def convolve_back(padded, kernel, dilation, flipped):
    out_rows = padded.shape[1] - 2 * dilation
    out_cols = padded.shape[2]
    pattern = 'oc,orw->crw' if flipped else 'co,orw->crw'
    summed = None
    for tap_index in range(9):
        window = window_at(padded, dilation, 2 - tap_index // 3, 2 - tap_index % 3, out_rows, out_cols)
        product = jnp.einsum(pattern, kernel[tap_index].astype(jnp.float32), window.astype(jnp.float32))
        summed = product if summed is None else summed + product
    return summed

def kernel_terms(padded_in, grad_out, dilation, flipped):
    out_rows = grad_out.shape[1]
    out_cols = grad_out.shape[2]
    pattern = 'crw,orw->oc' if flipped else 'crw,orw->co'
    listed = []
    for tap_index in range(9):
        window = window_at(padded_in, dilation, tap_index // 3, tap_index % 3, out_rows, out_cols)
        listed.append(jnp.einsum(pattern, window.astype(jnp.float32), grad_out.astype(jnp.float32)))
    return jnp.stack(listed)

def gelu_slope(preact, cotangent):
    return jax.vjp(jax.nn.gelu, preact)[1](cotangent)[0]

def advance(state, kernels):
    kernel_first, kernel_mid, kernel_last = kernels
    in_first = pad_rows(state, 1)
    pre_first = convolve(in_first, kernel_first, 1, False)
    hid_first = jax.nn.gelu(pre_first).astype(jnp.bfloat16)
    in_mid = pad_rows(hid_first, 2)
    pre_mid = convolve(in_mid, kernel_mid, 2, False)
    hid_mid = jax.nn.gelu(pre_mid).astype(jnp.bfloat16)
    in_last = pad_rows(hid_mid, 4)
    pre_last = convolve(in_last, kernel_last, 4, True)
    output = (state.astype(jnp.float32) + pre_last).astype(jnp.bfloat16)
    return (output, (in_first, in_mid, in_last, pre_first, pre_mid))

def backward(cot_out, saved, kernels):
    kernel_first, kernel_mid, kernel_last = kernels
    in_first, in_mid, in_last, pre_first, pre_mid = saved
    back_mid = convolve_back(pad_rows(cot_out, 4), kernel_last, 4, True)
    grads_last = kernel_terms(in_last, cot_out, 4, True)
    delta_mid = gelu_slope(pre_mid, back_mid).astype(jnp.bfloat16)
    back_first = convolve_back(pad_rows(delta_mid, 2), kernel_mid, 2, False)
    grads_mid = kernel_terms(in_mid, delta_mid, 2, False)
    delta_first = gelu_slope(pre_first, back_first).astype(jnp.bfloat16)
    back_state = convolve_back(pad_rows(delta_first, 1), kernel_first, 1, False)
    grads_first = kernel_terms(in_first, delta_first, 1, False)
    adjoint = (cot_out.astype(jnp.float32) + back_state).astype(jnp.bfloat16)
    return (adjoint, (grads_first, grads_mid, grads_last))

def reference(state_in, new_state, cot_early, cot_late, kernel_first, kernel_mid, kernel_last):
    kernels = (kernel_first, kernel_mid, kernel_last)

    def forward_only(state):
        return advance(state, kernels)[0]
    early = lax.map(forward_only, state_in)
    late_in = jnp.concatenate([new_state[None], early[:-1]], axis=0)

    def late_pass(pair):
        state, cotangent = pair
        output, saved = advance(state, kernels)
        adjoint, grads = backward(cotangent, saved, kernels)
        return (output, adjoint, grads)
    advanced, late_adj, late_grads = lax.map(late_pass, (late_in, cot_late))
    returned = jnp.concatenate([late_adj[1:], jnp.zeros_like(late_adj[:1])], axis=0)
    early_cot = (cot_early.astype(jnp.float32) + returned.astype(jnp.float32)).astype(jnp.bfloat16)

    def early_pass(pair):
        state, cotangent = pair
        output, saved = advance(state, kernels)
        return backward(cotangent, saved, kernels)
    state_adjoint, early_grads = lax.map(early_pass, (state_in, early_cot))
    grad_scale = 1.0 / math.sqrt(2.0 * STEPS * ROWS * COLS)
    grad_first = (lax.optimization_barrier(jnp.sum(late_grads[0], axis=0)) + lax.optimization_barrier(jnp.sum(early_grads[0], axis=0))) * grad_scale
    grad_mid = (lax.optimization_barrier(jnp.sum(late_grads[1], axis=0)) + lax.optimization_barrier(jnp.sum(early_grads[1], axis=0))) * grad_scale
    grad_last = (lax.optimization_barrier(jnp.sum(late_grads[2], axis=0)) + lax.optimization_barrier(jnp.sum(early_grads[2], axis=0))) * grad_scale
    return (advanced, state_adjoint, grad_first, grad_mid, grad_last)
```

```python
import functools
import math

import jax
import jax.numpy as jnp
from jax import lax
from jax.experimental import pallas as pl
from jax.experimental.pallas import tpu as pltpu
from jax.sharding import PartitionSpec as P

MESH = pl.DeviceIdType.MESH
BF = jnp.bfloat16
F32 = jnp.float32
HALO = 7
NT = (((1,), (1,)), ((), ()))


def gelu_pair(a):
    c0 = math.sqrt(2.0 / math.pi)
    c1 = c0 * 0.044715
    sq = a * a
    t = jnp.tanh(a * (c0 + c1 * sq))
    half = 0.5 + 0.5 * t
    slope = half + (a * (1.0 - t * t)) * (0.5 * c0 + (1.5 * c1) * sq)
    return a * half, slope


def shifted(piece, shift):
    width = piece.shape[1]
    if shift == 0:
        return piece
    column = lax.broadcasted_iota(jnp.int32, piece.shape, 1)
    moved = pltpu.roll(piece, (-shift) % width, 1)
    good = (column < width - shift) if shift > 0 else (column >= -shift)
    return jnp.where(good, moved, 0.0)


def spread(dst, value, lane, width, dilation, sign):
    channels = value.shape[0]
    for k in range(value.shape[1] // width):
        piece = value[:, k * width : (k + 1) * width]
        for j in range(3):
            moved = shifted(piece, sign * dilation * (j - 1))
            dst[j * channels : (j + 1) * channels, pl.ds(pl.multiple_of(lane + k * width, width), width)] = (
                moved.astype(BF)
            )


def gathered(total, width, dilation, sign):
    channels = total.shape[0] // 3
    rows = []
    for k in range(total.shape[1] // width):
        acc = None
        for j in (1, 0, 2):
            piece = total[j * channels : (j + 1) * channels, k * width : (k + 1) * width]
            moved = shifted(piece, sign * dilation * (j - 1))
            acc = moved if acc is None else acc + moved
        rows.append(acc)
    return jnp.concatenate(rows, axis=1)


def conv_chunk(weights, src, row, dilation, width, back):
    windows = []
    for i in range(3):
        offset = (2 - i if back else i) * dilation
        lane = pl.multiple_of((row + offset) * width, width)
        windows.append(src[:, pl.ds(lane, 2 * width)])
    return jnp.dot(weights[...], jnp.concatenate(windows, axis=0), preferred_element_type=F32)


def lay_out_forward(kf, km, kl, w1, w2, w3o):
    taps, ch, hid = kf.shape
    spare = w3o.shape[0] // 3 - ch

    def tall(kernel):
        block = [kernel[t].astype(F32) for t in range(taps)]
        if kernel.shape[1] == ch and spare:
            block = [jnp.concatenate([b, jnp.zeros((spare, hid), F32)], axis=0) for b in block]
        return block

    w1[...] = jnp.transpose(jnp.concatenate(tall(kf), axis=0)).astype(BF)
    w2[...] = jnp.transpose(jnp.concatenate(tall(km), axis=0)).astype(BF)
    last = tall(kl)
    for j in range(3):
        w3o[j * (ch + spare) : (j + 1) * (ch + spare), :] = jnp.concatenate(
            [last[3 * i + j] for i in range(3)], axis=1
        ).astype(BF)


def lay_out_backward(kf, km, kl, w1o, w2b, w3b):
    taps, ch, hid = kf.shape
    spare = w1o.shape[0] // 3 - ch

    def tall(kernel):
        block = [kernel[t].astype(F32) for t in range(taps)]
        if kernel.shape[1] == ch and spare:
            block = [jnp.concatenate([b, jnp.zeros((spare, hid), F32)], axis=0) for b in block]
        return block

    w3b[...] = jnp.transpose(jnp.concatenate(tall(kl), axis=0)).astype(BF)
    w2b[...] = jnp.concatenate(tall(km), axis=1).astype(BF)
    first = tall(kf)
    for j in range(3):
        w1o[j * (ch + spare) : (j + 1) * (ch + spare), :] = jnp.concatenate(
            [first[3 * i + j] for i in range(3)], axis=1
        ).astype(BF)


def mega_kernel(
    rows, width, steps, lats, piece, scale,
    state, new, late, early, kf, km, kl,
    adv, adj, packed,
    xs, xl, cl, ce, got, w1, w2, w3o, w1o, w2b, w3b,
    v3e, v3l, h1e, h1l, h2e, h2l, s1e, s1l, s2e, s2l, c3, g2s, g1, out_e, adj_l,
    tf, tm, tl, src, got_a, part_b, got_b, part_c, got_c, full, send, recv, send_r, recv_r,
):
    lat = lax.axis_index("lat")
    step = lax.axis_index("step")
    ch, band = state.shape
    cp, hid = xs.shape[0], w2.shape[0]
    edge, chunk = HALO * width, 2 * width
    pairs = steps // 2
    core = lax.rem(step, 2)
    pair = step // 2
    has_low, has_high = lat > 0, lat < lats - 1

    def lanes(row):
        return pl.ds(pl.multiple_of(row * width, width), chunk)

    def present(s, l):
        return (s >= 0) & (s < steps) & (l >= 0) & (l < lats)

    partner = {"step": pair * 2 + (1 - core)}

    def pair_peer(k):
        return {"step": lax.rem(pair + k, pairs) * 2 + core}

    def lat_peer(k):
        return {"lat": lax.rem(lat + k, lats)}

    barrier = pltpu.get_barrier_semaphore()
    always = [partner] + [pair_peer(k) for k in range(1, pairs)] + [lat_peer(k) for k in range(1, lats)]
    total = jnp.int32(len(always))
    for peer in always:
        pl.semaphore_signal(barrier, inc=1, device_id=peer, device_id_type=MESH)
    for s in (step - 1, step + 1):
        for l in (lat - 1, lat, lat + 1):
            there = present(s, l)

            @pl.when(there)
            def _(s=s, l=l):
                pl.semaphore_signal(barrier, inc=1, device_id={"step": s, "lat": l}, device_id_type=MESH)

            total = total + there.astype(jnp.int32)

    def place(wide, block):
        wide[:ch, edge : edge + band] = block[...]
        wide[ch:, edge : edge + band] = jnp.zeros((cp - ch, band), BF)

    def blank_edges(wide, low, high):
        @pl.when(low)
        def _():
            wide[:, :edge] = jnp.zeros((cp, edge), BF)

        @pl.when(high)
        def _():
            wide[:, edge + band :] = jnp.zeros((cp, edge), BF)

    def remote(source, target, k, peer):
        return pltpu.make_async_remote_copy(
            src_ref=source, dst_ref=target, send_sem=send.at[k], recv_sem=recv.at[k],
            device_id=peer, device_id_type=MESH,
        )

    def halo(wide, k):
        up = remote(wide.at[:, pl.ds(band, edge)], wide.at[:, pl.ds(0, edge)], k, {"lat": lat + 1})
        down = remote(wide.at[:, pl.ds(edge, edge)], wide.at[:, pl.ds(edge + band, edge)], k + 1, {"lat": lat - 1})
        return up, down

    def start_halo(pair_of, extra=None):
        up, down = pair_of
        pl.when(has_high if extra is None else has_high & extra)(up.start)
        pl.when(has_low if extra is None else has_low & extra)(down.start)

    def wait_halo(pair_of, extra=None):
        up, down = pair_of
        low = has_low if extra is None else has_low & extra
        high = has_high if extra is None else has_high & extra
        pl.when(low)(up.wait_recv)
        pl.when(high)(down.wait_recv)
        pl.when(high)(up.wait_send)
        pl.when(low)(down.wait_send)

    halo_state, halo_new, halo_late, halo_early = halo(xs, 0), halo(xl, 2), halo(cl, 4), halo(ce, 6)

    place(xs, state)
    blank_edges(xs, jnp.logical_not(has_low), jnp.logical_not(has_high))
    pl.semaphore_wait(barrier, total)
    start_halo(halo_state)
    first_step = step == 0

    @pl.when(first_step)
    def _():
        place(xl, new)

    start_halo(halo_new, first_step)
    blank_edges(xl, jnp.logical_not(has_low), jnp.logical_not(has_high))
    place(cl, late)
    blank_edges(cl, jnp.logical_not(has_low), jnp.logical_not(has_high))
    place(ce, early)
    blank_edges(ce, jnp.logical_not(has_low), jnp.logical_not(has_high))
    lay_out_forward(kf, km, kl, w1, w2, w3o)
    wait_halo(halo_state)
    start_halo(halo_late)

    def kept(value, row):
        pieces = []
        for k in range(2):
            g = lat * rows + (row + k - HALO)
            ok = (g >= 0) & (g < rows * lats)
            pieces.append(jnp.where(ok, value[:, k * width : (k + 1) * width], 0.0))
        return jnp.concatenate(pieces, axis=1)

    def forward(x, v3, h1, h2, s1, s2, out):
        @pl.loop(0, (rows + 14) // 2)
        def _(c):
            spread(v3, x[:, lanes(2 * c)].astype(F32), 2 * c * width, width, 1, 1)

        @pl.loop(0, (rows + 12) // 2, unroll=2)
        def _(c):
            value, slope = gelu_pair(conv_chunk(w1, v3, 2 * c, 1, width, False))
            s1[:, lanes(2 * c)] = slope.astype(BF)
            spread(h1, kept(value, 2 * c + 1), 2 * c * width, width, 2, 1)

        @pl.loop(0, (rows + 8) // 2, unroll=2)
        def _(c):
            value, slope = gelu_pair(conv_chunk(w2, h1, 2 * c, 2, width, False))
            s2[:, lanes(2 * c)] = slope.astype(BF)
            h2[:, lanes(2 * c)] = kept(value, 2 * c + 3).astype(BF)

        @pl.loop(0, rows // 2, unroll=2)
        def _(c):
            step_up = gathered(conv_chunk(w3o, h2, 2 * c, 4, width, False), width, 4, 1)
            base = x[:, lanes(2 * c + HALO)].astype(F32)
            out[:, lanes(2 * c)] = (base + step_up).astype(BF)

    def spread_cot(cot):
        @pl.loop(0, (rows + 14) // 2)
        def _(c):
            spread(c3, cot[:, lanes(2 * c)].astype(F32), 2 * c * width, width, 4, -1)

    def backward(cot, s1, s2, out):
        @pl.loop(0, (rows + 6) // 2)
        def _(c):
            total = conv_chunk(w3b, c3, 2 * c, 4, width, True)
            delta = s2[:, lanes(2 * c + 1)].astype(F32) * total
            spread(g2s, kept(delta, 2 * c + 4), 2 * c * width, width, 2, -1)

        @pl.loop(0, (rows + 2) // 2)
        def _(c):
            total = conv_chunk(w2b, g2s, 2 * c, 2, width, True)
            delta = s1[:, lanes(2 * c + 5)].astype(F32) * total
            g1[:, lanes(2 * c)] = kept(delta, 2 * c + 6).astype(BF)

        @pl.loop(0, rows // 2, unroll=2)
        def _(c):
            step_up = gathered(conv_chunk(w1o, g1, 2 * c, 1, width, True), width, 1, -1)
            base = cot[:, lanes(2 * c + HALO)].astype(F32)
            out[:, lanes(2 * c)] = (base + step_up).astype(BF)

    def nt(a, b):
        return lax.dot_general(a, b, NT, preferred_element_type=F32)

    def terms(v3, h1, h2, adds):
        @pl.loop(0, 3)
        def _(i):
            def window(row):
                return pl.ds(pl.multiple_of(row * width, width), band)

            last = nt(c3[:, window(3 + (2 - i) * 4)], h2[:, 4 * width : 4 * width + band])
            tl[i] = tl[i] + last if adds else last
            first = nt(v3[:, window(6 + i)], g1[:, width : width + band])
            tf[i] = tf[i] + first if adds else first
            for j in range(3):
                mid = nt(
                    h1[hid : 2 * hid, 6 * width : 6 * width + band],
                    g2s[j * hid : (j + 1) * hid, window(1 + (2 - i) * 2)],
                )
                tm[i, j] = tm[i, j] + mid if adds else mid

    def step_moves(block, target, distance, k):
        moves = []
        for n, (shift, source, into) in enumerate((
            (1, pl.ds(band - edge, edge), pl.ds(0, edge)),
            (0, pl.ds(0, band), pl.ds(edge, band)),
            (-1, pl.ds(0, edge), pl.ds(edge + band, edge)),
        )):
            made = remote(
                block.at[:, source], target.at[:, into], k + n, {"step": step + distance, "lat": lat + shift}
            )
            moves.append((present(step + distance, lat + shift), present(step - distance, lat - shift), into, made))
        return moves

    forward(xs, v3e, h1e, h2e, s1e, s2e, out_e)
    state_moves = step_moves(out_e, xl, 1, 8)
    for goes, comes, into, made in state_moves:
        pl.when(goes)(made.start)
    start_halo(halo_early)
    lay_out_backward(kf, km, kl, w1o, w2b, w3b)
    wait_halo(halo_late)
    spread_cot(cl)
    wait_halo(halo_new, first_step)
    for goes, comes, into, made in state_moves:
        pl.when(comes)(made.wait_recv)
    forward(xl, v3l, h1l, h2l, s1l, s2l, adv)
    backward(cl, s1l, s2l, adj_l)
    cot_moves = step_moves(adj_l, got, -1, 11)
    for goes, comes, into, made in cot_moves:
        pl.when(goes)(made.start)
    terms(v3l, h1l, h2l, False)
    wait_halo(halo_early)
    for goes, comes, into, made in state_moves:
        pl.when(goes)(made.wait_send)
    for goes, comes, into, made in cot_moves:
        @pl.when(comes)
        def _(into=into, made=made):
            made.wait_recv()
            ce[:, into] = (ce[:, into].astype(F32) + got[:, into].astype(F32)).astype(BF)

    spread_cot(ce)
    backward(ce, s1e, s2e, adj)
    terms(v3e, h1e, h2e, True)
    for goes, comes, into, made in cot_moves:
        pl.when(goes)(made.wait_send)

    half, wedge = pairs * lats * piece, lats * piece
    segments = got_a.shape[0]
    lane = src.shape[1]
    tap_rows = 3 * cp + hid + hid // 2

    @pl.loop(0, 3)
    def _(i):
        for j in range(3):
            start = pl.multiple_of((3 * i + j) * tap_rows, 16)
            first = tf[i, j * cp : (j + 1) * cp]
            last = tl[i, j * cp : (j + 1) * cp]
            mid = tm[i, j]
            src[pl.ds(start, cp), :] = first[:, :lane].astype(BF)
            src[pl.ds(start + cp, cp), :] = last[:, :lane].astype(BF)
            src[pl.ds(start + 2 * cp, cp), :] = jnp.concatenate([first[:, lane:], last[:, lane:]], axis=1).astype(BF)
            src[pl.ds(start + 3 * cp, hid), :] = mid[:, :lane].astype(BF)
            src[pl.ds(start + 3 * cp + hid, hid // 2), :] = jnp.concatenate(
                [mid[: hid // 2, lane:], mid[hid // 2 :, lane:]], axis=1
            ).astype(BF)

    used = 9 * tap_rows
    if used < src.shape[0]:
        src[used:, :] = jnp.zeros((src.shape[0] - used, lane), BF)

    count = [0]

    def rows_at(start, size):
        return pl.ds(pl.multiple_of(start, 16), size)

    def copy(source, target, peer):
        slot = count[0]
        count[0] += 1
        made = pltpu.make_async_remote_copy(
            src_ref=source, dst_ref=target, send_sem=send_r.at[slot], recv_sem=recv_r.at[slot],
            device_id=peer, device_id_type=MESH,
        )
        made.start()
        return made

    def finish(copies):
        for made in copies:
            made.wait()

    def stage_b(q):
        base = q * 2 * half + core * half
        for b in range(pairs):
            mine = src[rows_at(base + b * wedge, wedge), :].astype(F32)
            theirs = got_a[q, b * wedge : (b + 1) * wedge, :].astype(F32)
            part_b[q, b * wedge : (b + 1) * wedge, :] = (mine + theirs).astype(BF)
        return [
            copy(part_b.at[q, rows_at(lax.rem(pair + k, pairs) * wedge, wedge)], got_b.at[q, k - 1], pair_peer(k))
            for k in range(1, pairs)
        ]

    def stage_c(q):
        base = q * 2 * half + core * half + pair * wedge
        for c in range(lats):
            total = src[rows_at(base + c * piece, piece), :].astype(F32)
            total = total + got_a[q, rows_at(pair * wedge + c * piece, piece), :].astype(F32)
            for k in range(pairs - 1):
                total = total + got_b[q, k, c * piece : (c + 1) * piece, :].astype(F32)
            part_c[q, c * piece : (c + 1) * piece, :] = total.astype(BF)
        return [
            copy(part_c.at[q, rows_at(lax.rem(lat + k, lats) * piece, piece)], got_c.at[q, k - 1], lat_peer(k))
            for k in range(1, lats)
        ]

    def spread_c(q):
        total = part_c[q, rows_at(lat * piece, piece), :].astype(F32)
        for k in range(lats - 1):
            total = total + got_c[q, k].astype(F32)
        mine = rows_at(q * 2 * half + core * half + pair * wedge + lat * piece, piece)
        full[mine, :] = (total * scale).astype(BF)
        return [copy(full.at[mine], full.at[mine], lat_peer(k)) for k in range(1, lats)]

    def spread_b(q):
        held = full.at[rows_at(q * 2 * half + core * half + pair * wedge, wedge)]
        return [copy(held, held, pair_peer(k)) for k in range(1, pairs)]

    def spread_a(q):
        held = full.at[rows_at(q * 2 * half + core * half, half)]
        return [copy(held, held, partner)]

    flying = [
        [copy(src.at[rows_at(q * 2 * half + (1 - core) * half, half)], got_a.at[q], partner)]
        for q in range(segments)
    ]
    for stage in (stage_b, stage_c, spread_c, spread_b, spread_a):
        for q in range(segments):
            finish(flying[q])
            flying[q] = stage(q)
    for q in range(segments):
        finish(flying[q])
    packed[...] = full[...]


def unpack_kernel(packed, out_first, out_mid, out_last):
    ch, hid = out_first.shape[1:]
    lane = packed.shape[1]
    rest = hid - lane
    cp = (packed.shape[0] - hid - hid // 2) // 3
    tails = packed[2 * cp : 3 * cp, :].astype(F32)
    out_first[0, :, :lane] = packed[:cp, :].astype(F32)[:ch]
    out_first[0, :, lane:] = tails[:ch, :rest]
    out_last[0, :, :lane] = packed[cp : 2 * cp, :].astype(F32)[:ch]
    out_last[0, :, lane:] = tails[:ch, rest:]
    tails = packed[3 * cp + hid :, :].astype(F32)
    out_mid[0, :, :lane] = packed[3 * cp : 3 * cp + hid, :].astype(F32)
    out_mid[0, : hid // 2, lane:] = tails[:, :rest]
    out_mid[0, hid // 2 :, lane:] = tails[:, rest:]


def body(state_in, new_state, cot_early, cot_late, kernel_first, kernel_mid, kernel_last):
    steps, lats = lax.axis_size("step"), lax.axis_size("lat")
    ch, rows, width = new_state.shape
    hid = kernel_mid.shape[1]
    taps = kernel_mid.shape[0]
    cp = -(-ch // 16) * 16
    band, edge = rows * width, HALO * width
    pairs = steps // 2
    pieces = steps * lats
    lane = 128
    tap_rows = 3 * cp + hid + hid // 2
    segments = 2
    piece = -(-taps * tap_rows // (segments * pieces * 16)) * 16
    packed_rows = segments * pieces * piece
    copies = segments * (2 + 2 * (pairs - 1) + 2 * (lats - 1))
    scale = 1.0 / math.sqrt(2.0 * steps * rows * lats * width)

    vmem = pl.BlockSpec(memory_space=pltpu.VMEM)
    shape = jax.ShapeDtypeStruct
    lanes_v, lanes_1, lanes_2 = (rows + 14) * width, (rows + 12) * width, (rows + 8) * width
    wide = ((cp, lanes_v), BF)
    scratch = [wide] * 5 + [
        ((hid, 9 * cp), BF), ((hid, 9 * hid), BF), ((3 * cp, 3 * hid), BF),
        ((3 * cp, 3 * hid), BF), ((hid, 9 * hid), BF), ((hid, 9 * cp), BF),
        ((3 * cp, lanes_v), BF), ((3 * cp, lanes_v), BF),
        ((3 * hid, lanes_1), BF), ((3 * hid, lanes_1), BF),
        ((hid, lanes_2), BF), ((hid, lanes_2), BF),
        ((hid, lanes_1), BF), ((hid, lanes_1), BF),
        ((hid, lanes_2), BF), ((hid, lanes_2), BF),
        ((3 * cp, lanes_v), BF), ((3 * hid, (rows + 6) * width), BF), ((hid, (rows + 2) * width), BF),
        ((cp, band), BF), ((cp, band), BF),
        ((3, 3 * cp, hid), F32), ((3, 3, hid, hid), F32), ((3, 3 * cp, hid), F32),
        ((packed_rows, lane), BF),
        ((segments, pairs * lats * piece, lane), BF),
        ((segments, pairs * lats * piece, lane), BF),
        ((segments, max(pairs - 1, 1), lats * piece, lane), BF),
        ((segments, lats * piece, lane), BF),
        ((segments, max(lats - 1, 1), piece, lane), BF),
        ((packed_rows, lane), BF),
    ]
    advanced, adjoint, packed = pl.pallas_call(
        functools.partial(mega_kernel, rows, width, steps, lats, piece, scale),
        out_shape=[shape((cp, band), BF), shape((cp, band), BF), shape((packed_rows, lane), BF)],
        in_specs=[vmem] * 7,
        out_specs=[vmem] * 3,
        scratch_shapes=[pltpu.VMEM(*s) for s in scratch] + [
            pltpu.SemaphoreType.DMA((14,)), pltpu.SemaphoreType.DMA((14,)),
            pltpu.SemaphoreType.DMA((copies,)), pltpu.SemaphoreType.DMA((copies,)),
        ],
        compiler_params=pltpu.CompilerParams(
            collective_id=0, has_side_effects=True, vmem_limit_bytes=60 * 1024 * 1024
        ),
        name="rollout",
    )(
        *(block.reshape(ch, band) for block in (state_in[0], new_state, cot_late[0], cot_early[0])),
        kernel_first, kernel_mid, kernel_last,
    )
    first, mid, last = pl.pallas_call(
        unpack_kernel,
        grid=(taps,),
        out_shape=[shape((taps, ch, hid), F32), shape((taps, hid, hid), F32), shape((taps, ch, hid), F32)],
        in_specs=[pl.BlockSpec((tap_rows, lane), lambda t: (t, 0))],
        out_specs=[
            pl.BlockSpec((1, ch, hid), lambda t: (t, 0, 0)),
            pl.BlockSpec((1, hid, hid), lambda t: (t, 0, 0)),
            pl.BlockSpec((1, ch, hid), lambda t: (t, 0, 0)),
        ],
        name="unpack_terms",
    )(packed)
    return (
        advanced[:ch].reshape(1, ch, rows, width),
        adjoint[:ch].reshape(1, ch, rows, width),
        first,
        mid,
        last,
    )


def solution(mesh):
    banded = P("step", None, "lat", None)
    return jax.shard_map(
        body,
        mesh=mesh,
        in_specs=(banded, P(None, "lat", None), banded, banded, P(), P(), P()),
        out_specs=(banded, banded, P(), P(), P()),
        check_vma=False,
    )
```

```python
import functools
import math

import jax
import jax.numpy as jnp
from jax import lax
from jax.experimental import pallas as pl
from jax.experimental.pallas import tpu as pltpu
from jax.sharding import PartitionSpec as P

MESH = pl.DeviceIdType.MESH
BF = jnp.bfloat16
F32 = jnp.float32
HALO = 7
NT = (((1,), (1,)), ((), ()))


def gelu_pair(a):
    c0 = math.sqrt(2.0 / math.pi)
    c1 = c0 * 0.044715
    sq = a * a
    t = jnp.tanh(a * (c0 + c1 * sq))
    half = 0.5 + 0.5 * t
    slope = half + (a * (1.0 - t * t)) * (0.5 * c0 + (1.5 * c1) * sq)
    return a * half, slope


def row_pair(src, row, offsets):
    return jnp.concatenate(
        [jnp.concatenate([src[row + k + o] for o in offsets], axis=0) for k in range(2)], axis=1
    )


def shifted(value, shift):
    width = value.shape[1]
    if shift == 0:
        return value
    column = lax.broadcasted_iota(jnp.int32, value.shape, 1)
    moved = pltpu.roll(value, (-shift) % width, 1)
    good = (column < width - shift) if shift > 0 else (column >= -shift)
    return jnp.where(good, moved, 0.0)


def put_spread(dst, row, value, dilation, sign):
    channels = value.shape[0]
    for j in range(3):
        dst[row, j * channels : (j + 1) * channels, :] = shifted(value, sign * dilation * (j - 1)).astype(BF)


def gathered(total, dilation, sign):
    channels = total.shape[0] // 3
    acc = total[channels : 2 * channels]
    for j in (0, 2):
        acc = acc + shifted(total[j * channels : (j + 1) * channels], sign * dilation * (j - 1))
    return acc


def each(count, work, unroll=None):
    pl.loop(0, count, unroll=count if unroll is None else unroll)(work)


def dot(a, b):
    return jnp.dot(a, b, preferred_element_type=F32)


def nt(a, b):
    return lax.dot_general(a, b, NT, preferred_element_type=F32)


def side(src, row, count, low, high):
    return jnp.concatenate([src[row + k, low:high] for k in range(count)], axis=1)


def tall(kernel, spare):
    taps, _, hid = kernel.shape
    block = [kernel[t].astype(F32) for t in range(taps)]
    if spare:
        block = [jnp.concatenate([b, jnp.zeros((spare, hid), F32)], axis=0) for b in block]
    return block


def lay_out_across(kernel, out, spare):
    out[...] = jnp.transpose(jnp.concatenate(tall(kernel, spare), axis=0)).astype(BF)


def lay_out_along(kernel, out):
    out[...] = jnp.concatenate(tall(kernel, 0), axis=1).astype(BF)


def lay_out_stacked(kernel, out, spare):
    blocks = tall(kernel, spare)
    size = blocks[0].shape[0]
    for j in range(3):
        out[j * size : (j + 1) * size, :] = jnp.concatenate(
            [blocks[3 * i + j] for i in range(3)], axis=1
        ).astype(BF)


def pack_terms(blocks, lane, size):
    rest = blocks[0].shape[1] - lane
    main = jnp.concatenate([b[:, :lane] for b in blocks], axis=0)
    tails = jnp.concatenate([b[:, lane:] for b in blocks], axis=0)
    count = main.shape[0]
    cut = half_rows(count)
    low = tails[cut:]
    if cut * 2 > count:
        low = jnp.concatenate([low, jnp.zeros((2 * cut - count, rest), F32)], axis=0)
    parts = [main, jnp.concatenate([tails[:cut], low], axis=1)]
    if size > count + cut:
        parts.append(jnp.zeros((size - count - cut, lane), F32))
    return jnp.concatenate(parts, axis=0).astype(BF)


def half_rows(count):
    return -(-count // 16) * 8


class Plan:
    def __init__(self, steps, lats, ch, hid):
        devices = steps * lats
        self.lane = 128
        taps = 9
        small = taps * ch + half_rows(taps * ch)
        self.mid_tap = hid + hid // 2
        mid = taps * self.mid_tap
        self.small = -(-small // 16) * 16
        piece_last = -(-self.small // (16 * devices)) * 16
        piece_mid = max(1, mid // (16 * devices)) * 16
        self.last = 0
        self.mid = piece_last * devices
        edge = self.mid + piece_mid * devices
        self.first = max(self.mid + mid, edge)
        piece_first = -(-(self.first + self.small - edge) // (16 * devices)) * 16
        self.gap = (self.mid + mid, self.first)
        self.rows = edge + piece_first * devices
        self.pieces = (piece_last, piece_mid, piece_first)
        self.bases = (self.last, self.mid, edge)


def mega_kernel(
    rows, width, steps, lats, scale, plan,
    state, new, late, early, kf, km, kl,
    adv, adj, full,
    xs, xl, cl, ce, got, w1, w2, w3o, w1o, w2b, w3b,
    v3e, v3l, h1e, h1l, h2e, h2l, s1e, s1l, s2e, c3, g2s, g1, b2, out_e, adj_l,
    tf, tm, tl, src, *rest,
):
    buffers = [rest[5 * q : 5 * q + 5] for q in range(3)]
    send, recv, send_r, recv_r = rest[15:]
    lat = lax.axis_index("lat")
    step = lax.axis_index("step")
    ch = state.shape[1]
    cp, hid = xs.shape[1], w2.shape[0]
    spare = cp - ch
    ext = rows + 2 * HALO
    pairs = steps // 2
    core = lax.rem(step, 2)
    pair = step // 2
    has_low, has_high = lat > 0, lat < lats - 1
    first_step = step == 0

    def present(s, l):
        return (s >= 0) & (s < steps) & (l >= 0) & (l < lats)

    partner = {"step": pair * 2 + (1 - core)}

    def pair_peer(k):
        return {"step": lax.rem(pair + k, pairs) * 2 + core}

    def lat_peer(k):
        return {"lat": lax.rem(lat + k, lats)}

    barrier = pltpu.get_barrier_semaphore()
    always = [partner] + [pair_peer(k) for k in range(1, pairs)] + [lat_peer(k) for k in range(1, lats)]
    total = jnp.int32(len(always))
    for peer in always:
        pl.semaphore_signal(barrier, inc=1, device_id=peer, device_id_type=MESH)
    for s in (step - 1, step + 1):
        for l in (lat - 1, lat, lat + 1):
            there = present(s, l)

            @pl.when(there)
            def _(s=s, l=l):
                pl.semaphore_signal(barrier, inc=1, device_id={"step": s, "lat": l}, device_id_type=MESH)

            total = total + there.astype(jnp.int32)

    def place(wide, block):
        value = jnp.swapaxes(block.astype(F32), 0, 1)
        value = jnp.concatenate([value, jnp.zeros((rows, spare, width), F32)], axis=1)
        wide[HALO : HALO + rows] = value.astype(BF)

    def blank_edges(wide):
        @pl.when(jnp.logical_not(has_low))
        def _():
            wide[:HALO] = jnp.zeros((HALO, cp, width), BF)

        @pl.when(jnp.logical_not(has_high))
        def _():
            wide[HALO + rows :] = jnp.zeros((HALO, cp, width), BF)

    def remote(source, target, k, peer):
        return pltpu.make_async_remote_copy(
            src_ref=source, dst_ref=target, send_sem=send.at[k], recv_sem=recv.at[k],
            device_id=peer, device_id_type=MESH,
        )

    def halo(wide, k):
        up = remote(wide.at[pl.ds(rows, HALO)], wide.at[pl.ds(0, HALO)], k, {"lat": lat + 1})
        down = remote(wide.at[pl.ds(HALO, HALO)], wide.at[pl.ds(HALO + rows, HALO)], k + 1, {"lat": lat - 1})
        return up, down

    def start_halo(both, extra=None):
        up, down = both
        pl.when(has_high if extra is None else has_high & extra)(up.start)
        pl.when(has_low if extra is None else has_low & extra)(down.start)

    def wait_halo(both, extra=None):
        up, down = both
        low = has_low if extra is None else has_low & extra
        high = has_high if extra is None else has_high & extra
        pl.when(low)(up.wait_recv)
        pl.when(high)(down.wait_recv)
        pl.when(high)(up.wait_send)
        pl.when(low)(down.wait_send)

    def kept(value, row):
        g = lat * rows + (row - HALO)
        return jnp.where((g >= 0) & (g < rows * lats), value, 0.0)

    def halves(total):
        return total[:, :width], total[:, width:]

    def spread_rows(wide, dst, first, count, dilation, sign):
        each(count, lambda r: put_spread(dst, first + r, wide[first + r].astype(F32), dilation, sign))

    def conv1(v3, s1, h1, row):
        for k, part in enumerate(halves(dot(w1[...], row_pair(v3, row, (0, 1, 2))))):
            value, slope = gelu_pair(part)
            s1[row + k] = slope.astype(BF)
            put_spread(h1, row + k, kept(value, row + k + 1), 2, 1)

    def conv2(h1, h2, row):
        result = []
        for k, part in enumerate(halves(dot(w2[...], row_pair(h1, row, (0, 2, 4))))):
            value, slope = gelu_pair(part)
            h2[row + k] = kept(value, row + k + 3).astype(BF)
            result.append(slope)
        return result

    def conv3(x, h2, out, row):
        for k, part in enumerate(halves(dot(w3o[...], row_pair(h2, row, (0, 4, 8))))):
            out[row + k] = (x[row + k + HALO].astype(F32) + gathered(part, 4, 1)).astype(BF)

    def back1(s1, row):
        for k, part in enumerate(halves(dot(w2b[...], row_pair(g2s, row, (4, 2, 0))))):
            delta = s1[row + k + 5].astype(F32) * part
            g1[row + k] = kept(delta, row + k + 6).astype(BF)

    def back0(cot, out, row):
        for k, part in enumerate(halves(dot(w1o[...], row_pair(g1, row, (2, 1, 0))))):
            out[row + k] = (cot[row + k + HALO].astype(F32) + gathered(part, 1, -1)).astype(BF)

    def put_g2(row, delta):
        put_spread(g2s, row, kept(delta, row + 4), 2, -1)

    def last_term(h2, i):
        return nt(side(c3, 3 + (2 - i) * 4, rows, 0, 3 * cp), side(h2, 4, rows, 0, hid))

    def first_term(v3, i):
        return nt(side(v3, 6 + i, rows, 0, 3 * cp), side(g1, 1, rows, 0, hid))

    def mid_term(h1, i, j):
        return nt(side(h1, 6, rows, hid, 2 * hid), side(g2s, 1 + (2 - i) * 2, rows, j * hid, (j + 1) * hid))

    half_band = rows // 2

    def step_moves(block, target, distance, k):
        groups = []
        for group in (
            ((-1, 0, HALO, HALO + rows), (0, 0, half_band, HALO)),
            ((1, rows - HALO, HALO, 0), (0, half_band, rows - half_band, HALO + half_band)),
        ):
            moves = []
            for shift, source, count, into in group:
                made = remote(
                    block.at[pl.ds(source, count)], target.at[pl.ds(into, count)], k,
                    {"step": step + distance, "lat": lat + shift},
                )
                k += 1
                moves.append((present(step + distance, lat + shift), present(step - distance, lat - shift), into, count, made))
            groups.append(moves)
        return groups

    def start_moves(moves):
        for goes, comes, into, size, made in moves:
            pl.when(goes)(made.start)

    halo_state, halo_new, halo_late, halo_early = halo(xs, 0), halo(xl, 2), halo(cl, 4), halo(ce, 6)
    state_low, state_high = step_moves(out_e, xl, 1, 8)
    cot_low, cot_high = step_moves(adj_l, got, -1, 12)

    place(xs, state[0])
    blank_edges(xs)
    pl.semaphore_wait(barrier, total)
    start_halo(halo_state)
    pl.when(first_step)(lambda: place(xl, new[...]))
    start_halo(halo_new, first_step)
    blank_edges(xl)
    lay_out_across(kf, w1, spare)
    spread_rows(xs, v3e, HALO, rows, 1, 1)
    inner_first = HALO + 1
    inner_pairs = (rows - 4) // 2
    each(inner_pairs, lambda c: conv1(v3e, s1e, h1e, inner_first + 2 * c))
    place(cl, late[0])
    blank_edges(cl)
    place(ce, early[0])
    blank_edges(ce)
    lay_out_across(km, w2, 0)
    lay_out_stacked(kl, w3o, spare)
    wait_halo(halo_state)
    start_halo(halo_late)
    spread_rows(xs, v3e, 0, HALO, 1, 1)
    spread_rows(xs, v3e, HALO + rows, HALO, 1, 1)
    low_pairs = inner_first // 2
    each(low_pairs, lambda c: conv1(v3e, s1e, h1e, 2 * c))
    high_first = inner_first + 2 * inner_pairs
    each((rows + 12 - high_first) // 2, lambda c: conv1(v3e, s1e, h1e, high_first + 2 * c))

    def early_conv2(c):
        for k, slope in enumerate(conv2(h1e, h2e, 2 * c)):
            s2e[2 * c + k] = slope.astype(BF)

    each((rows + 8) // 2, early_conv2)
    each(half_band // 2, lambda c: conv3(xs, h2e, out_e, 2 * c))
    start_moves(state_low)
    each((rows - half_band) // 2, lambda c: conv3(xs, h2e, out_e, half_band + 2 * c))
    start_moves(state_high)
    start_halo(halo_early)

    lay_out_across(kl, w3b, spare)
    lay_out_along(km, w2b)
    lay_out_stacked(kf, w1o, spare)
    wait_halo(halo_late)
    spread_rows(cl, c3, 0, ext, 4, -1)

    def late_back2(c):
        for k, part in enumerate(halves(dot(w3b[...], row_pair(c3, 2 * c, (8, 4, 0))))):
            b2[2 * c + k] = part

    each((rows + 6) // 2, late_back2)
    wait_halo(halo_new, first_step)
    for goes, comes, into, size, made in state_low + state_high:
        pl.when(comes)(made.wait_recv)
    spread_rows(xl, v3l, 0, ext, 1, 1)
    each((rows + 12) // 2, lambda c: conv1(v3l, s1l, h1l, 2 * c))

    def late_conv2(row):
        for k, slope in enumerate(conv2(h1l, h2l, row)):
            r = row + k - 1
            put_g2(r, slope * b2[r])

    conv2_first = conv2(h1l, h2l, 0)
    put_g2(0, conv2_first[1] * b2[0])
    each((rows + 4) // 2, lambda c: late_conv2(2 * c + 2))
    conv2_last = conv2(h1l, h2l, rows + 6)
    put_g2(rows + 5, conv2_last[0] * b2[rows + 5])
    each((rows + 2) // 2, lambda c: back1(s1l, 2 * c))
    each(half_band // 2, lambda c: back0(cl, adj_l, 2 * c))
    start_moves(cot_low)
    each((rows - half_band) // 2, lambda c: back0(cl, adj_l, half_band + 2 * c))
    start_moves(cot_high)

    @pl.loop(0, 3)
    def _(i):
        tl[i] = last_term(h2l, i)
        for j in range(3):
            tm[i, j] = mid_term(h1l, i, j)
        tf[i] = first_term(v3l, i)

    wait_halo(halo_early)
    for goes, comes, into, size, made in cot_low + cot_high:
        @pl.when(comes)
        def _(into=into, size=size, made=made):
            made.wait_recv()
            for r in range(into, into + size):
                ce[r] = (ce[r].astype(F32) + got[r].astype(F32)).astype(BF)

    slots = [0]

    def rows_at(start, size):
        return pl.ds(pl.multiple_of(start, 16), size)

    def copy(source, target, peer):
        slot = slots[0]
        slots[0] += 1
        made = pltpu.make_async_remote_copy(
            src_ref=source, dst_ref=target, send_sem=send_r.at[slot], recv_sem=recv_r.at[slot],
            device_id=peer, device_id_type=MESH,
        )
        made.start()
        return made

    def summing(q):
        piece, base = plan.pieces[q], plan.bases[q]
        got_a, part_b, got_b, part_c, got_c = buffers[q]
        half, wedge = pairs * lats * piece, lats * piece
        mine_half = base + core * half
        flying = [copy(src.at[rows_at(base + (1 - core) * half, half)], got_a, partner)]

        def finish():
            for made in flying:
                made.wait()

        yield
        finish()
        part_b[...] = (src[rows_at(mine_half, half), :].astype(F32) + got_a[...].astype(F32)).astype(BF)
        flying = [
            copy(part_b.at[rows_at(lax.rem(pair + k, pairs) * wedge, wedge)], got_b.at[k - 1], pair_peer(k))
            for k in range(1, pairs)
        ]
        yield
        finish()
        total = src[rows_at(mine_half + pair * wedge, wedge), :].astype(F32)
        total = total + got_a[rows_at(pair * wedge, wedge), :].astype(F32)
        for k in range(pairs - 1):
            total = total + got_b[k].astype(F32)
        part_c[...] = total.astype(BF)
        flying = [
            copy(part_c.at[rows_at(lax.rem(lat + k, lats) * piece, piece)], got_c.at[k - 1], lat_peer(k))
            for k in range(1, lats)
        ]
        yield
        finish()
        total = part_c[rows_at(lat * piece, piece), :].astype(F32)
        for k in range(lats - 1):
            total = total + got_c[k].astype(F32)
        mine = rows_at(mine_half + pair * wedge + lat * piece, piece)
        full[mine, :] = (total * scale).astype(BF)
        flying = [copy(full.at[mine], full.at[mine], lat_peer(k)) for k in range(1, lats)]
        yield
        finish()
        held = full.at[rows_at(mine_half + pair * wedge, wedge)]
        flying = [copy(held, held, pair_peer(k)) for k in range(1, pairs)]
        yield
        finish()
        held = full.at[rows_at(mine_half, half)]
        flying = [copy(held, held, partner)]
        yield
        finish()
        yield

    def blocks_of(terms):
        return [terms[i, j * cp : j * cp + ch] for i in range(3) for j in range(3)]

    lane = plan.lane

    spread_rows(ce, c3, 0, ext, 4, -1)

    @pl.loop(0, 3)
    def _(i):
        tl[i] = tl[i] + last_term(h2e, i)

    src[: plan.mid, :] = pack_terms(blocks_of(tl), lane, plan.mid)
    sum_last = summing(0)
    next(sum_last)

    def early_back2(c):
        for k, part in enumerate(halves(dot(w3b[...], row_pair(c3, 2 * c, (8, 4, 0))))):
            row = 2 * c + k
            put_g2(row, s2e[row + 1].astype(F32) * part)

    each((rows + 6) // 2, early_back2)
    next(sum_last)

    @pl.loop(0, 3)
    def _(i):
        for j in range(3):
            start = pl.multiple_of(plan.mid + (3 * i + j) * plan.mid_tap, 16)
            src[pl.ds(start, plan.mid_tap), :] = pack_terms([tm[i, j] + mid_term(h1e, i, j)], lane, plan.mid_tap)

    if plan.gap[1] > plan.gap[0]:
        src[plan.gap[0] : plan.gap[1], :] = jnp.zeros((plan.gap[1] - plan.gap[0], lane), BF)
    sum_mid = summing(1)
    next(sum_mid)
    next(sum_last)
    each((rows + 2) // 2, lambda c: back1(s1e, 2 * c))
    next(sum_mid)
    next(sum_last)

    @pl.loop(0, 3)
    def _(i):
        tf[i] = tf[i] + first_term(v3e, i)

    src[plan.first :, :] = pack_terms(blocks_of(tf), lane, plan.rows - plan.first)
    sum_first = summing(2)
    next(sum_first)
    next(sum_mid)
    next(sum_last)
    each(rows // 2, lambda c: back0(ce, adj, 2 * c))
    next(sum_first)
    next(sum_last)
    next(sum_mid)
    each(rows // 2, lambda c: conv3(xl, h2l, adv, 2 * c))
    next(sum_first)
    next(sum_mid)
    next(sum_last)
    next(sum_first)
    next(sum_mid)
    next(sum_first)
    next(sum_mid)
    next(sum_first)
    next(sum_first)

    for goes, comes, into, size, made in state_low + state_high + cot_low + cot_high:
        pl.when(goes)(made.wait_send)


def unpack_kernel(plan, adv, adj, packed, out_adv, out_adj, out_first, out_mid, out_last):
    taps, ch, hid = out_first.shape
    lane = plan.lane
    rest = hid - lane
    for source, target in ((adv, out_adv), (adj, out_adj)):
        target[0] = jnp.swapaxes(source[...].astype(F32), 0, 1)[:ch].astype(BF)
    for start, out in ((plan.last, out_last), (plan.first, out_first)):
        count = taps * ch
        cut = half_rows(count)
        value = packed[start : start + plan.small, :].astype(F32)
        tails = value[count : count + cut]
        tails = jnp.concatenate([tails[:, :rest], tails[:, rest:]], axis=0)
        for t in range(taps):
            out[t, :, :lane] = value[t * ch : (t + 1) * ch]
            out[t, :, lane:] = tails[t * ch : (t + 1) * ch]

    @pl.loop(0, taps)
    def _(t):
        start = pl.multiple_of(plan.mid + t * plan.mid_tap, 16)
        value = packed[pl.ds(start, plan.mid_tap), :].astype(F32)
        cut = half_rows(hid)
        out_mid[t, :, :lane] = value[:hid]
        out_mid[t, :cut, lane:] = value[hid : hid + cut, :rest]
        out_mid[t, cut:, lane:] = value[hid : hid + cut, rest:]


def body(state_in, new_state, cot_early, cot_late, kernel_first, kernel_mid, kernel_last):
    steps, lats = lax.axis_size("step"), lax.axis_size("lat")
    ch, rows, width = new_state.shape
    hid = kernel_mid.shape[1]
    taps = kernel_mid.shape[0]
    cp = -(-ch // 16) * 16
    pairs = steps // 2
    plan = Plan(steps, lats, ch, hid)
    lane = plan.lane
    copies = 3 * (2 + 2 * (pairs - 1) + 2 * (lats - 1))
    scale = 1.0 / math.sqrt(2.0 * steps * rows * lats * width)

    vmem = pl.BlockSpec(memory_space=pltpu.VMEM)
    shape = jax.ShapeDtypeStruct
    ext, ext_1, ext_2 = rows + 14, rows + 12, rows + 8
    scratch = [((ext, cp, width), BF)] * 5 + [
        ((hid, 9 * cp), BF), ((hid, 9 * hid), BF), ((3 * cp, 3 * hid), BF),
        ((3 * cp, 3 * hid), BF), ((hid, 9 * hid), BF), ((hid, 9 * cp), BF),
        ((ext, 3 * cp, width), BF), ((ext, 3 * cp, width), BF),
        ((ext_1, 3 * hid, width), BF), ((ext_1, 3 * hid, width), BF),
        ((ext_2, hid, width), BF), ((ext_2, hid, width), BF),
        ((ext_1, hid, width), BF), ((ext_1, hid, width), BF),
        ((ext_2, hid, width), BF),
        ((ext, 3 * cp, width), BF), ((rows + 6, 3 * hid, width), BF), ((rows + 2, hid, width), BF),
        ((rows + 6, hid, width), F32),
        ((rows, cp, width), BF), ((rows, cp, width), BF),
        ((3, 3 * cp, hid), F32), ((3, 3, hid, hid), F32), ((3, 3 * cp, hid), F32),
        ((plan.rows, lane), BF),
    ]
    for piece in plan.pieces:
        half, wedge = pairs * lats * piece, lats * piece
        scratch += [
            ((half, lane), BF), ((half, lane), BF), ((max(pairs - 1, 1), wedge, lane), BF),
            ((wedge, lane), BF), ((max(lats - 1, 1), piece, lane), BF),
        ]
    sems = pltpu.SemaphoreType.DMA
    band_shape = shape((rows, cp, width), BF)
    advanced, adjoint, packed = pl.pallas_call(
        functools.partial(mega_kernel, rows, width, steps, lats, scale, plan),
        out_shape=[band_shape, band_shape, shape((plan.rows, lane), BF)],
        in_specs=[vmem] * 7,
        out_specs=[vmem] * 3,
        scratch_shapes=[pltpu.VMEM(*s) for s in scratch] + [sems((16,)), sems((16,)), sems((copies,)), sems((copies,))],
        compiler_params=pltpu.CompilerParams(
            collective_id=0, has_side_effects=True, vmem_limit_bytes=60 * 1024 * 1024
        ),
        name="rollout",
    )(state_in, new_state, cot_late, cot_early, kernel_first, kernel_mid, kernel_last)
    return pl.pallas_call(
        functools.partial(unpack_kernel, plan),
        out_shape=[
            shape((1, ch, rows, width), BF), shape((1, ch, rows, width), BF),
            shape((taps, ch, hid), F32), shape((taps, hid, hid), F32), shape((taps, ch, hid), F32),
        ],
        in_specs=[vmem] * 3,
        out_specs=[vmem] * 5,
        compiler_params=pltpu.CompilerParams(vmem_limit_bytes=32 * 1024 * 1024),
        name="unpack_terms",
    )(advanced, adjoint, packed)


def solution(mesh):
    banded = P("step", None, "lat", None)
    return jax.shard_map(
        body,
        mesh=mesh,
        in_specs=(banded, P(None, "lat", None), banded, banded, P(), P(), P()),
        out_specs=(banded, banded, P(), P(), P()),
        check_vma=False,
    )
```

```python
import functools
import math

import jax
import jax.numpy as jnp
from jax import lax
from jax.experimental import pallas as pl
from jax.experimental.pallas import tpu as pltpu
from jax.sharding import PartitionSpec as P

MESH = pl.DeviceIdType.MESH
BF = jnp.bfloat16
F32 = jnp.float32
HALO = 7
NT = (((1,), (1,)), ((), ()))


def gelu_pair(a):
    c0 = math.sqrt(2.0 / math.pi)
    c1 = c0 * 0.044715
    sq = a * a
    t = jnp.tanh(a * (c0 + c1 * sq))
    half = 0.5 + 0.5 * t
    slope = half + (a * (1.0 - t * t)) * (0.5 * c0 + (1.5 * c1) * sq)
    return a * half, slope


def row_pair(src, row, offsets):
    return jnp.concatenate(
        [jnp.concatenate([src[row + k + o] for o in offsets], axis=0) for k in range(2)], axis=1
    )


def shifted(value, shift):
    width = value.shape[1]
    if shift == 0:
        return value
    column = lax.broadcasted_iota(jnp.int32, value.shape, 1)
    moved = pltpu.roll(value, (-shift) % width, 1)
    good = (column < width - shift) if shift > 0 else (column >= -shift)
    return jnp.where(good, moved, 0.0)


def put_spread(dst, row, value, dilation, sign):
    channels = value.shape[0]
    for j in range(3):
        dst[row, j * channels : (j + 1) * channels, :] = shifted(value, sign * dilation * (j - 1)).astype(BF)


def gathered(total, dilation, sign):
    channels = total.shape[0] // 3
    acc = total[channels : 2 * channels]
    for j in (0, 2):
        acc = acc + shifted(total[j * channels : (j + 1) * channels], sign * dilation * (j - 1))
    return acc


def each(count, work, unroll=None):
    pl.loop(0, count, unroll=count if unroll is None else unroll)(work)


def dot(a, b):
    return jnp.dot(a, b, preferred_element_type=F32)


def nt(a, b):
    return lax.dot_general(a, b, NT, preferred_element_type=F32)


def side(src, row, count, low, high):
    return jnp.concatenate([src[row + k, low:high] for k in range(count)], axis=1)


def tall(kernel, spare):
    taps, _, hid = kernel.shape
    block = [kernel[t].astype(F32) for t in range(taps)]
    if spare:
        block = [jnp.concatenate([b, jnp.zeros((spare, hid), F32)], axis=0) for b in block]
    return block


def lay_out_across(kernel, out, spare):
    out[...] = jnp.transpose(jnp.concatenate(tall(kernel, spare), axis=0)).astype(BF)


def lay_out_along(kernel, out):
    out[...] = jnp.concatenate(tall(kernel, 0), axis=1).astype(BF)


def lay_out_stacked(kernel, out, spare):
    blocks = tall(kernel, spare)
    size = blocks[0].shape[0]
    for j in range(3):
        out[j * size : (j + 1) * size, :] = jnp.concatenate(
            [blocks[3 * i + j] for i in range(3)], axis=1
        ).astype(BF)


def pack_terms(blocks, lane, size):
    rest = blocks[0].shape[1] - lane
    main = jnp.concatenate([b[:, :lane] for b in blocks], axis=0)
    tails = jnp.concatenate([b[:, lane:] for b in blocks], axis=0)
    count = main.shape[0]
    cut = half_rows(count)
    low = tails[cut:]
    if cut * 2 > count:
        low = jnp.concatenate([low, jnp.zeros((2 * cut - count, rest), F32)], axis=0)
    parts = [main, jnp.concatenate([tails[:cut], low], axis=1)]
    if size > count + cut:
        parts.append(jnp.zeros((size - count - cut, lane), F32))
    return jnp.concatenate(parts, axis=0).astype(BF)


def half_rows(count):
    return -(-count // 16) * 8


class Plan:
    def __init__(self, steps, lats, ch, hid):
        devices = steps * lats
        unit = 16 * devices
        self.lane = 128
        taps = 9
        small = taps * ch + half_rows(taps * ch)
        self.mid_tap = hid + hid // 2
        mid = taps * self.mid_tap
        self.small = -(-small // 16) * 16
        self.last = 0
        last_units = -(-self.small // unit)
        self.mid = last_units * unit
        units = max(1, mid // unit)
        groups = min(3, units)
        edge = self.mid
        direct = devices <= 32
        self.segments = [(self.last, 16 * last_units, direct)]
        self.taps_ready = []
        for k in range(groups):
            size = units // groups + (k < units % groups)
            self.segments.append((edge, 16 * size, False))
            edge += size * unit
            ready = min(taps, -(-(edge - self.mid) // self.mid_tap))
            self.taps_ready.append(taps if k == groups - 1 else ready)
        self.first = max(self.mid + mid, edge)
        first_units = -(-(self.first + self.small - edge) // unit)
        self.segments.append((edge, 16 * first_units, direct))
        self.gap = (self.mid + mid, self.first)
        self.rows = edge + first_units * unit
        chips = devices // 2
        pairs = steps // 2
        self.shapes, self.slots = [], 0
        for _, piece, direct in self.segments:
            half, wedge = chips * piece, lats * piece
            if direct:
                self.shapes.append([(half,), (half,), (max(chips - 1, 1), piece)])
                self.slots += 2 + 2 * (chips - 1)
            else:
                self.shapes.append([
                    (half,), (half,), (max(pairs - 1, 1), wedge), (wedge,), (max(lats - 1, 1), piece),
                ])
                self.slots += 2 + 2 * (pairs - 1) + 2 * (lats - 1)


def mega_kernel(
    rows, width, steps, lats, scale, plan,
    state, new, late, early, kf, km, kl,
    adv, adj, full,
    xs, xl, cl, ce, got, w1, w2, w3o, w1o, w2b, w3b,
    v3e, v3l, h1e, h1l, h2e, h2l, s1e, s1l, s2e, c3, g2s, g1, b2, out_e, adj_l,
    tf, tm, tl, src, *rest,
):
    buffers = []
    for dims in plan.shapes:
        buffers.append(rest[: len(dims)])
        rest = rest[len(dims) :]
    send, recv, send_r, recv_r = rest
    lat = lax.axis_index("lat")
    step = lax.axis_index("step")
    ch = state.shape[1]
    cp, hid = xs.shape[1], w2.shape[0]
    spare = cp - ch
    ext = rows + 2 * HALO
    pairs = steps // 2
    core = lax.rem(step, 2)
    pair = step // 2
    has_low, has_high = lat > 0, lat < lats - 1
    first_step = step == 0

    def present(s, l):
        return (s >= 0) & (s < steps) & (l >= 0) & (l < lats)

    partner = {"step": pair * 2 + (1 - core)}

    def pair_peer(k):
        return {"step": lax.rem(pair + k, pairs) * 2 + core}

    def lat_peer(k):
        return {"lat": lax.rem(lat + k, lats)}

    def chip_peer(k, n):
        return {"step": lax.rem(pair + k, pairs) * 2 + core, "lat": lax.rem(lat + n, lats)}

    others = [(k, n) for k in range(pairs) for n in range(lats) if k or n]

    barrier = pltpu.get_barrier_semaphore()
    always = [partner]
    if any(direct for _, _, direct in plan.segments):
        always += [chip_peer(k, n) for k, n in others]
    else:
        always += [pair_peer(k) for k in range(1, pairs)] + [lat_peer(k) for k in range(1, lats)]
    total = jnp.int32(len(always))
    for peer in always:
        pl.semaphore_signal(barrier, inc=1, device_id=peer, device_id_type=MESH)
    for s in (step - 1, step + 1):
        for l in (lat - 1, lat, lat + 1):
            there = present(s, l)

            @pl.when(there)
            def _(s=s, l=l):
                pl.semaphore_signal(barrier, inc=1, device_id={"step": s, "lat": l}, device_id_type=MESH)

            total = total + there.astype(jnp.int32)

    def place(wide, block):
        value = jnp.swapaxes(block.astype(F32), 0, 1)
        value = jnp.concatenate([value, jnp.zeros((rows, spare, width), F32)], axis=1)
        wide[HALO : HALO + rows] = value.astype(BF)

    def blank_edges(wide):
        @pl.when(jnp.logical_not(has_low))
        def _():
            wide[:HALO] = jnp.zeros((HALO, cp, width), BF)

        @pl.when(jnp.logical_not(has_high))
        def _():
            wide[HALO + rows :] = jnp.zeros((HALO, cp, width), BF)

    def remote(source, target, k, peer):
        return pltpu.make_async_remote_copy(
            src_ref=source, dst_ref=target, send_sem=send.at[k], recv_sem=recv.at[k],
            device_id=peer, device_id_type=MESH,
        )

    def halo(wide, k):
        up = remote(wide.at[pl.ds(rows, HALO)], wide.at[pl.ds(0, HALO)], k, {"lat": lat + 1})
        down = remote(wide.at[pl.ds(HALO, HALO)], wide.at[pl.ds(HALO + rows, HALO)], k + 1, {"lat": lat - 1})
        return up, down

    def start_halo(both, extra=None):
        up, down = both
        pl.when(has_high if extra is None else has_high & extra)(up.start)
        pl.when(has_low if extra is None else has_low & extra)(down.start)

    def wait_halo(both, extra=None):
        up, down = both
        low = has_low if extra is None else has_low & extra
        high = has_high if extra is None else has_high & extra
        pl.when(low)(up.wait_recv)
        pl.when(high)(down.wait_recv)
        pl.when(high)(up.wait_send)
        pl.when(low)(down.wait_send)

    def kept(value, row):
        g = lat * rows + (row - HALO)
        return jnp.where((g >= 0) & (g < rows * lats), value, 0.0)

    def halves(total):
        return total[:, :width], total[:, width:]

    def spread_rows(wide, dst, first, count, dilation, sign):
        each(count, lambda r: put_spread(dst, first + r, wide[first + r].astype(F32), dilation, sign))

    def conv1(v3, s1, h1, row):
        for k, part in enumerate(halves(dot(w1[...], row_pair(v3, row, (0, 1, 2))))):
            value, slope = gelu_pair(part)
            s1[row + k] = slope.astype(BF)
            put_spread(h1, row + k, kept(value, row + k + 1), 2, 1)

    def conv2(h1, h2, row):
        result = []
        for k, part in enumerate(halves(dot(w2[...], row_pair(h1, row, (0, 2, 4))))):
            value, slope = gelu_pair(part)
            h2[row + k] = kept(value, row + k + 3).astype(BF)
            result.append(slope)
        return result

    def conv3(x, h2, out, row):
        for k, part in enumerate(halves(dot(w3o[...], row_pair(h2, row, (0, 4, 8))))):
            out[row + k] = (x[row + k + HALO].astype(F32) + gathered(part, 4, 1)).astype(BF)

    def back1(s1, row):
        for k, part in enumerate(halves(dot(w2b[...], row_pair(g2s, row, (4, 2, 0))))):
            delta = s1[row + k + 5].astype(F32) * part
            g1[row + k] = kept(delta, row + k + 6).astype(BF)

    def back0(cot, out, row):
        for k, part in enumerate(halves(dot(w1o[...], row_pair(g1, row, (2, 1, 0))))):
            out[row + k] = (cot[row + k + HALO].astype(F32) + gathered(part, 1, -1)).astype(BF)

    def put_g2(row, delta):
        put_spread(g2s, row, kept(delta, row + 4), 2, -1)

    def last_term(h2, i):
        return nt(side(c3, 3 + (2 - i) * 4, rows, 0, 3 * cp), side(h2, 4, rows, 0, hid))

    def first_term(v3, i):
        return nt(side(v3, 6 + i, rows, 0, 3 * cp), side(g1, 1, rows, 0, hid))

    def mid_term(h1, i, j):
        return nt(side(h1, 6, rows, hid, 2 * hid), side(g2s, 1 + (2 - i) * 2, rows, j * hid, (j + 1) * hid))

    half_band = rows // 2

    def step_moves(block, target, distance, k):
        groups = []
        for group in (
            ((0, 0, half_band, HALO), (-1, 0, HALO, HALO + rows)),
            ((0, half_band, rows - half_band, HALO + half_band), (1, rows - HALO, HALO, 0)),
        ):
            moves = []
            for shift, source, count, into in group:
                made = remote(
                    block.at[pl.ds(source, count)], target.at[pl.ds(into, count)], k,
                    {"step": step + distance, "lat": lat + shift},
                )
                k += 1
                moves.append((present(step + distance, lat + shift), present(step - distance, lat - shift), into, count, made))
            groups.append(moves)
        return groups

    def start_moves(moves):
        for goes, comes, into, size, made in moves:
            pl.when(goes)(made.start)

    halo_state, halo_new, halo_late, halo_early = halo(xs, 0), halo(xl, 2), halo(cl, 4), halo(ce, 6)
    state_low, state_high = step_moves(out_e, xl, 1, 8)
    cot_low, cot_high = step_moves(adj_l, got, -1, 12)

    place(xs, state[0])
    blank_edges(xs)
    pl.semaphore_wait(barrier, total)
    start_halo(halo_state)
    pl.when(first_step)(lambda: place(xl, new[...]))
    start_halo(halo_new, first_step)
    blank_edges(xl)
    lay_out_across(kf, w1, spare)
    spread_rows(xs, v3e, HALO, rows, 1, 1)
    inner_first = HALO + 1
    inner_pairs = (rows - 4) // 2
    each(inner_pairs, lambda c: conv1(v3e, s1e, h1e, inner_first + 2 * c))
    lay_out_across(km, w2, 0)

    def early_conv2(row):
        for k, slope in enumerate(conv2(h1e, h2e, row)):
            s2e[row + k] = slope.astype(BF)

    each(inner_pairs - 2, lambda c: early_conv2(inner_first + 2 * c))
    place(cl, late[0])
    blank_edges(cl)
    place(ce, early[0])
    blank_edges(ce)
    lay_out_stacked(kl, w3o, spare)
    wait_halo(halo_state)
    start_halo(halo_late)
    spread_rows(xs, v3e, 0, HALO, 1, 1)
    spread_rows(xs, v3e, HALO + rows, HALO, 1, 1)
    low_pairs = inner_first // 2
    each(low_pairs, lambda c: conv1(v3e, s1e, h1e, 2 * c))
    high_first = inner_first + 2 * inner_pairs
    each((rows + 12 - high_first) // 2, lambda c: conv1(v3e, s1e, h1e, high_first + 2 * c))

    each(low_pairs, lambda c: early_conv2(2 * c))
    each(low_pairs, lambda c: early_conv2(high_first - 4 + 2 * c))
    each(half_band // 2, lambda c: conv3(xs, h2e, out_e, 2 * c))
    start_moves(state_low)
    each((rows - half_band) // 2, lambda c: conv3(xs, h2e, out_e, half_band + 2 * c))
    start_moves(state_high)
    start_halo(halo_early)

    lay_out_across(kl, w3b, spare)
    lay_out_along(km, w2b)
    lay_out_stacked(kf, w1o, spare)
    wait_halo(halo_late)
    spread_rows(cl, c3, 0, ext, 4, -1)

    def late_back2(c):
        for k, part in enumerate(halves(dot(w3b[...], row_pair(c3, 2 * c, (8, 4, 0))))):
            b2[2 * c + k] = part

    each((rows + 6) // 2, late_back2)
    def late_conv2(row):
        for k, slope in enumerate(conv2(h1l, h2l, row)):
            r = row + k - 1
            put_g2(r, slope * b2[r])

    state_moves, cot_moves = state_low + state_high, cot_low + cot_high
    for goes, comes, into, size, made in (state_moves[0], state_moves[2]):
        pl.when(comes)(made.wait_recv)
    spread_rows(xl, v3l, HALO, rows, 1, 1)
    each(inner_pairs, lambda c: conv1(v3l, s1l, h1l, inner_first + 2 * c))
    each(inner_pairs - 2, lambda c: late_conv2(inner_first + 2 * c))
    wait_halo(halo_new, first_step)
    for goes, comes, into, size, made in (state_moves[1], state_moves[3]):
        pl.when(comes)(made.wait_recv)
    spread_rows(xl, v3l, 0, HALO, 1, 1)
    spread_rows(xl, v3l, HALO + rows, HALO, 1, 1)
    each(low_pairs, lambda c: conv1(v3l, s1l, h1l, 2 * c))
    each((rows + 12 - high_first) // 2, lambda c: conv1(v3l, s1l, h1l, high_first + 2 * c))
    conv2_first = conv2(h1l, h2l, 0)
    put_g2(0, conv2_first[1] * b2[0])
    each(low_pairs - 1, lambda c: late_conv2(2 * c + 2))
    each(low_pairs - 1, lambda c: late_conv2(high_first - 4 + 2 * c))
    conv2_last = conv2(h1l, h2l, rows + 6)
    put_g2(rows + 5, conv2_last[0] * b2[rows + 5])
    each((rows + 2) // 2, lambda c: back1(s1l, 2 * c))
    each(half_band // 2, lambda c: back0(cl, adj_l, 2 * c))
    start_moves(cot_low)
    each((rows - half_band) // 2, lambda c: back0(cl, adj_l, half_band + 2 * c))
    start_moves(cot_high)

    @pl.loop(0, 3)
    def _(i):
        tl[i] = last_term(h2l, i)
        for j in range(3):
            tm[i, j] = mid_term(h1l, i, j)
        tf[i] = first_term(v3l, i)

    wait_halo(halo_early)
    def add_cot(moves):
        for goes, comes, into, size, made in moves:
            @pl.when(comes)
            def _(into=into, size=size, made=made):
                made.wait_recv()
                for r in range(into, into + size):
                    ce[r] = (ce[r].astype(F32) + got[r].astype(F32)).astype(BF)

    add_cot((cot_moves[0], cot_moves[2]))
    spread_rows(ce, c3, HALO, rows, 4, -1)
    add_cot((cot_moves[1], cot_moves[3]))
    spread_rows(ce, c3, 0, HALO, 4, -1)
    spread_rows(ce, c3, HALO + rows, HALO, 4, -1)

    slots = [0]

    def rows_at(start, size):
        return pl.ds(pl.multiple_of(start, 16), size)

    def copy(source, target, peer):
        slot = slots[0]
        slots[0] += 1
        made = pltpu.make_async_remote_copy(
            src_ref=source, dst_ref=target, send_sem=send_r.at[slot], recv_sem=recv_r.at[slot],
            device_id=peer, device_id_type=MESH,
        )
        made.start()
        return made

    def summing_direct(q):
        base, piece, _ = plan.segments[q]
        got_a, part, got_b = buffers[q]
        half = pairs * lats * piece
        mine_half = base + core * half
        me = pair * lats + lat
        made = copy(src.at[rows_at(base + (1 - core) * half, half)], got_a, partner)
        yield
        made.wait()
        part[...] = (src[rows_at(mine_half, half), :].astype(F32) + got_a[...].astype(F32)).astype(BF)
        flying = []
        for slot, (k, n) in enumerate(others):
            place_of = lax.rem(pair + k, pairs) * lats + lax.rem(lat + n, lats)
            flying.append(copy(part.at[rows_at(place_of * piece, piece)], got_b.at[slot], chip_peer(k, n)))
        yield
        for made in flying:
            made.wait()
        total = src[rows_at(mine_half + me * piece, piece), :].astype(F32)
        total = total + got_a[rows_at(me * piece, piece), :].astype(F32)
        for slot in range(len(others)):
            total = total + got_b[slot].astype(F32)
        mine = rows_at(mine_half + me * piece, piece)
        full[mine, :] = (total * scale).astype(BF)
        flying = [copy(full.at[mine], full.at[mine], chip_peer(k, n)) for k, n in others]
        yield
        for made in flying:
            made.wait()
        held = full.at[rows_at(mine_half, half)]
        made = copy(held, held, partner)
        yield
        made.wait()
        yield

    def summing(q):
        base, piece, direct = plan.segments[q]
        if direct:
            yield from summing_direct(q)
            return
        got_a, part_b, got_b, part_c, got_c = buffers[q]
        half, wedge = pairs * lats * piece, lats * piece
        mine_half = base + core * half
        flying = [copy(src.at[rows_at(base + (1 - core) * half, half)], got_a, partner)]

        def finish():
            for made in flying:
                made.wait()

        yield
        finish()
        part_b[...] = (src[rows_at(mine_half, half), :].astype(F32) + got_a[...].astype(F32)).astype(BF)
        flying = [
            copy(part_b.at[rows_at(lax.rem(pair + k, pairs) * wedge, wedge)], got_b.at[k - 1], pair_peer(k))
            for k in range(1, pairs)
        ]
        yield
        finish()
        total = src[rows_at(mine_half + pair * wedge, wedge), :].astype(F32)
        total = total + got_a[rows_at(pair * wedge, wedge), :].astype(F32)
        for k in range(pairs - 1):
            total = total + got_b[k].astype(F32)
        part_c[...] = total.astype(BF)
        flying = [
            copy(part_c.at[rows_at(lax.rem(lat + k, lats) * piece, piece)], got_c.at[k - 1], lat_peer(k))
            for k in range(1, lats)
        ]
        yield
        finish()
        total = part_c[rows_at(lat * piece, piece), :].astype(F32)
        for k in range(lats - 1):
            total = total + got_c[k].astype(F32)
        mine = rows_at(mine_half + pair * wedge + lat * piece, piece)
        full[mine, :] = (total * scale).astype(BF)
        flying = [copy(full.at[mine], full.at[mine], lat_peer(k)) for k in range(1, lats)]
        yield
        finish()
        held = full.at[rows_at(mine_half + pair * wedge, wedge)]
        flying = [copy(held, held, pair_peer(k)) for k in range(1, pairs)]
        yield
        finish()
        held = full.at[rows_at(mine_half, half)]
        flying = [copy(held, held, partner)]
        yield
        finish()
        yield

    def blocks_of(terms):
        return [terms[i, j * cp : j * cp + ch] for i in range(3) for j in range(3)]

    lane = plan.lane

    sums = [summing(q) for q in range(len(plan.segments))]
    sum_last, sum_mids, sum_first = sums[0], sums[1:-1], sums[-1]

    def advance(*which):
        for one in which:
            next(one, None)

    def early_back2(c):
        for k, part in enumerate(halves(dot(w3b[...], row_pair(c3, 2 * c, (8, 4, 0))))):
            row = 2 * c + k
            put_g2(row, s2e[row + 1].astype(F32) * part)

    each((rows + 6) // 2, early_back2)
    tap = 0
    for k, ready in enumerate(plan.taps_ready):
        for t in range(tap, ready):
            value = tm[t // 3, t % 3] + mid_term(h1e, t // 3, t % 3)
            start = plan.mid + t * plan.mid_tap
            src[start : start + plan.mid_tap, :] = pack_terms([value], lane, plan.mid_tap)
        tap = ready
        if tap == 9 and plan.gap[1] > plan.gap[0]:
            src[plan.gap[0] : plan.gap[1], :] = jnp.zeros((plan.gap[1] - plan.gap[0], lane), BF)
        advance(sum_mids[k])
        if k == 1:
            advance(sum_mids[0])

    @pl.loop(0, 3)
    def _(i):
        tl[i] = tl[i] + last_term(h2e, i)

    src[: plan.mid, :] = pack_terms(blocks_of(tl), lane, plan.mid)
    advance(sum_last, *sum_mids[1:])
    each((rows + 2) // 2, lambda c: back1(s1e, 2 * c))
    advance(sum_last)

    @pl.loop(0, 3)
    def _(i):
        tf[i] = tf[i] + first_term(v3e, i)

    src[plan.first :, :] = pack_terms(blocks_of(tf), lane, plan.rows - plan.first)
    advance(sum_first, sum_mids[0])
    each(rows // 2, lambda c: back0(ce, adj, 2 * c))
    advance(sum_first, *sum_mids[1:])
    each(rows // 2, lambda c: conv3(xl, h2l, adv, 2 * c))
    advance(sum_mids[0], sum_last, *sum_mids[1:])
    advance(sum_first, *sum_mids)
    advance(sum_last, sum_mids[0], sum_first, *sum_mids[1:])
    for _ in range(7):
        advance(sum_last, *sum_mids, sum_first)

    for goes, comes, into, size, made in state_moves + cot_moves:
        pl.when(goes)(made.wait_send)


def unpack_kernel(plan, adv, adj, packed, out_adv, out_adj, out_first, out_mid, out_last):
    taps, ch, hid = out_first.shape
    lane = plan.lane
    rest = hid - lane
    for source, target in ((adv, out_adv), (adj, out_adj)):
        target[0] = jnp.swapaxes(source[...].astype(F32), 0, 1)[:ch].astype(BF)
    for start, out in ((plan.last, out_last), (plan.first, out_first)):
        count = taps * ch
        cut = half_rows(count)
        value = packed[start : start + plan.small, :].astype(F32)
        tails = value[count : count + cut]
        tails = jnp.concatenate([tails[:, :rest], tails[:, rest:]], axis=0)
        for t in range(taps):
            out[t, :, :lane] = value[t * ch : (t + 1) * ch]
            out[t, :, lane:] = tails[t * ch : (t + 1) * ch]

    @pl.loop(0, taps)
    def _(t):
        start = pl.multiple_of(plan.mid + t * plan.mid_tap, 16)
        value = packed[pl.ds(start, plan.mid_tap), :].astype(F32)
        cut = half_rows(hid)
        out_mid[t, :, :lane] = value[:hid]
        out_mid[t, :cut, lane:] = value[hid : hid + cut, :rest]
        out_mid[t, cut:, lane:] = value[hid : hid + cut, rest:]


def body(state_in, new_state, cot_early, cot_late, kernel_first, kernel_mid, kernel_last):
    steps, lats = lax.axis_size("step"), lax.axis_size("lat")
    ch, rows, width = new_state.shape
    hid = kernel_mid.shape[1]
    taps = kernel_mid.shape[0]
    cp = -(-ch // 16) * 16
    plan = Plan(steps, lats, ch, hid)
    lane = plan.lane
    scale = 1.0 / math.sqrt(2.0 * steps * rows * lats * width)

    vmem = pl.BlockSpec(memory_space=pltpu.VMEM)
    shape = jax.ShapeDtypeStruct
    ext, ext_1, ext_2 = rows + 14, rows + 12, rows + 8
    scratch = [((ext, cp, width), BF)] * 5 + [
        ((hid, 9 * cp), BF), ((hid, 9 * hid), BF), ((3 * cp, 3 * hid), BF),
        ((3 * cp, 3 * hid), BF), ((hid, 9 * hid), BF), ((hid, 9 * cp), BF),
        ((ext, 3 * cp, width), BF), ((ext, 3 * cp, width), BF),
        ((ext_1, 3 * hid, width), BF), ((ext_1, 3 * hid, width), BF),
        ((ext_2, hid, width), BF), ((ext_2, hid, width), BF),
        ((ext_1, hid, width), BF), ((ext_1, hid, width), BF),
        ((ext_2, hid, width), BF),
        ((ext, 3 * cp, width), BF), ((rows + 6, 3 * hid, width), BF), ((rows + 2, hid, width), BF),
        ((rows + 6, hid, width), F32),
        ((rows, cp, width), BF), ((rows, cp, width), BF),
        ((3, 3 * cp, hid), F32), ((3, 3, hid, hid), F32), ((3, 3 * cp, hid), F32),
        ((plan.rows, lane), BF),
    ]
    for dims in plan.shapes:
        scratch += [(d + (lane,), BF) for d in dims]
    sems = pltpu.SemaphoreType.DMA
    band_shape = shape((rows, cp, width), BF)
    advanced, adjoint, packed = pl.pallas_call(
        functools.partial(mega_kernel, rows, width, steps, lats, scale, plan),
        out_shape=[band_shape, band_shape, shape((plan.rows, lane), BF)],
        in_specs=[vmem] * 7,
        out_specs=[vmem] * 3,
        scratch_shapes=[pltpu.VMEM(*s) for s in scratch] + [sems((16,)), sems((16,)), sems((plan.slots,)), sems((plan.slots,))],
        compiler_params=pltpu.CompilerParams(
            collective_id=0, has_side_effects=True, vmem_limit_bytes=60 * 1024 * 1024
        ),
        name="rollout",
    )(state_in, new_state, cot_late, cot_early, kernel_first, kernel_mid, kernel_last)
    return pl.pallas_call(
        functools.partial(unpack_kernel, plan),
        out_shape=[
            shape((1, ch, rows, width), BF), shape((1, ch, rows, width), BF),
            shape((taps, ch, hid), F32), shape((taps, hid, hid), F32), shape((taps, ch, hid), F32),
        ],
        in_specs=[vmem] * 3,
        out_specs=[vmem] * 5,
        compiler_params=pltpu.CompilerParams(vmem_limit_bytes=60 * 1024 * 1024),
        name="unpack_terms",
    )(advanced, adjoint, packed)


def solution(mesh):
    banded = P("step", None, "lat", None)
    return jax.shard_map(
        body,
        mesh=mesh,
        in_specs=(banded, P(None, "lat", None), banded, banded, P(), P(), P()),
        out_specs=(banded, banded, P(), P(), P()),
        check_vma=False,
    )
```

```python
import functools
import math

import jax
import jax.numpy as jnp
from jax import lax
from jax.experimental import pallas as pl
from jax.experimental.pallas import tpu as pltpu
from jax.sharding import PartitionSpec as P

MESH = pl.DeviceIdType.MESH
BF = jnp.bfloat16
F32 = jnp.float32
HALO = 7
NT = (((1,), (1,)), ((), ()))


def gelu_pair(a):
    c0 = math.sqrt(2.0 / math.pi)
    c1 = c0 * 0.044715
    sq = a * a
    t = jnp.tanh(a * (c0 + c1 * sq))
    half = 0.5 + 0.5 * t
    slope = half + (a * (1.0 - t * t)) * (0.5 * c0 + (1.5 * c1) * sq)
    return a * half, slope


def row_pair(src, row, offsets):
    return jnp.concatenate(
        [jnp.concatenate([src[row + k + o] for o in offsets], axis=0) for k in range(2)], axis=1
    )


def shifted(value, shift):
    width = value.shape[1]
    if shift == 0:
        return value
    column = lax.broadcasted_iota(jnp.int32, value.shape, 1)
    moved = pltpu.roll(value, (-shift) % width, 1)
    good = (column < width - shift) if shift > 0 else (column >= -shift)
    return jnp.where(good, moved, 0.0)


def put_spread(dst, row, value, dilation, sign):
    channels, pitch = value.shape[0], dst.shape[1] // 3
    for j in range(3):
        dst[row, j * pitch : j * pitch + channels, :] = shifted(value, sign * dilation * (j - 1)).astype(BF)


def gathered(total, dilation, sign):
    channels = total.shape[0] // 3
    acc = total[channels : 2 * channels]
    for j in (0, 2):
        acc = acc + shifted(total[j * channels : (j + 1) * channels], sign * dilation * (j - 1))
    return acc


def each(count, work, unroll=None):
    pl.loop(0, count, unroll=count if unroll is None else unroll)(work)


def dot(a, b):
    return jnp.dot(a, b, preferred_element_type=F32)


def nt(a, b):
    return lax.dot_general(a, b, NT, preferred_element_type=F32)


def side(src, row, count, low, high):
    return jnp.concatenate([src[row + k, low:high] for k in range(count)], axis=1)


def tall(kernel, spare):
    taps, _, hid = kernel.shape
    block = [kernel[t].astype(F32) for t in range(taps)]
    if spare:
        block = [jnp.concatenate([b, jnp.zeros((spare, hid), F32)], axis=0) for b in block]
    return block


def lay_out_across(kernel, out, spare):
    out[...] = jnp.transpose(jnp.concatenate(tall(kernel, spare), axis=0)).astype(BF)


def lay_out_along(kernel, out):
    out[...] = jnp.concatenate(tall(kernel, 0), axis=1).astype(BF)


def lay_out_stacked(kernel, out, spare):
    blocks = tall(kernel, spare)
    size = blocks[0].shape[0]
    for j in range(3):
        out[j * size : (j + 1) * size, :] = jnp.concatenate(
            [blocks[3 * i + j] for i in range(3)], axis=1
        ).astype(BF)


def pack_terms(blocks, lane, size):
    rest = blocks[0].shape[1] - lane
    main = jnp.concatenate([b[:, :lane] for b in blocks], axis=0)
    tails = jnp.concatenate([b[:, lane:] for b in blocks], axis=0)
    count = main.shape[0]
    cut = half_rows(count)
    low = tails[cut:]
    if cut * 2 > count:
        low = jnp.concatenate([low, jnp.zeros((2 * cut - count, rest), F32)], axis=0)
    parts = [main, jnp.concatenate([tails[:cut], low], axis=1)]
    if size > count + cut:
        parts.append(jnp.zeros((size - count - cut, lane), F32))
    return jnp.concatenate(parts, axis=0).astype(BF)


def half_rows(count):
    return -(-count // 16) * 8


class Plan:
    def __init__(self, steps, lats, ch, hid):
        devices = steps * lats
        unit = 16 * devices
        self.lane = 128
        taps = 9
        small = taps * ch + half_rows(taps * ch)
        self.mid_tap = hid + hid // 2
        mid = taps * self.mid_tap
        self.small = -(-small // 16) * 16
        self.last = 0
        last_units = -(-self.small // unit)
        self.mid = last_units * unit
        units = max(1, mid // unit)
        groups = min(3, units)
        edge = self.mid
        direct = devices <= 32
        self.segments = [(self.last, 16 * last_units, direct)]
        self.taps_ready = []
        for k in range(groups):
            size = units // groups + (k < units % groups)
            self.segments.append((edge, 16 * size, False))
            edge += size * unit
            ready = min(taps, -(-(edge - self.mid) // self.mid_tap))
            self.taps_ready.append(taps if k == groups - 1 else ready)
        self.first = max(self.mid + mid, edge)
        first_units = -(-(self.first + self.small - edge) // unit)
        self.segments.append((edge, 16 * first_units, direct))
        self.gap = (self.mid + mid, self.first)
        self.rows = edge + first_units * unit
        chips = devices // 2
        pairs = steps // 2
        self.shapes, self.slots = [], 0
        for _, piece, direct in self.segments:
            half, wedge = chips * piece, lats * piece
            if direct:
                self.shapes.append([(half,), (half,), (max(chips - 1, 1), piece)])
                self.slots += 2 + 2 * (chips - 1)
            else:
                self.shapes.append([
                    (half,), (half,), (max(pairs - 1, 1), wedge), (wedge,), (max(lats - 1, 1), piece),
                ])
                self.slots += 2 + 2 * (pairs - 1) + 2 * (lats - 1)


def mega_kernel(
    rows, width, steps, lats, scale, plan,
    state_in, new_in, late_in, early_in, kf_in, km_in, kl_in,
    adv_out, adj_out, packed,
    state, new, late, early, kf, km, kl, adv, adj, full, load, store,
    xs, xl, cl, ce, got, w1, w2, w3o, w1o, w2b, w3b,
    v3e, v3l, h1e, h1l, h2e, h2l, s1e, s1l, s2e, c3, g2s, g1, b2, out_e, adj_l,
    tf, tm, tl, src, *rest,
):
    buffers = []
    for dims in plan.shapes:
        buffers.append(rest[: len(dims)])
        rest = rest[len(dims) :]
    send, recv, send_r, recv_r = rest
    lat = lax.axis_index("lat")
    step = lax.axis_index("step")
    ch = xs.shape[1]
    cp, hid = c3.shape[1] // 3, w2.shape[0]
    spare = cp - ch
    ext = rows + 2 * HALO
    pairs = steps // 2
    core = lax.rem(step, 2)
    pair = step // 2
    has_low, has_high = lat > 0, lat < lats - 1
    first_step = step == 0

    def present(s, l):
        return (s >= 0) & (s < steps) & (l >= 0) & (l < lats)

    partner = {"step": pair * 2 + (1 - core)}

    def pair_peer(k):
        return {"step": lax.rem(pair + k, pairs) * 2 + core}

    def lat_peer(k):
        return {"lat": lax.rem(lat + k, lats)}

    def chip_peer(k, n):
        return {"step": lax.rem(pair + k, pairs) * 2 + core, "lat": lax.rem(lat + n, lats)}

    others = [(k, n) for k in range(pairs) for n in range(lats) if k or n]

    loads = {}
    for n, (name, source, target) in enumerate((
        ("state", state_in.at[0], state), ("kf", kf_in, kf), ("new", new_in, new), ("km", km_in, km),
        ("late", late_in.at[0], late), ("early", early_in.at[0], early), ("kl", kl_in, kl),
    )):
        loads[name] = pltpu.make_async_copy(source, target, load.at[n])
        loads[name].start()
    stores = []

    def keep(source, target):
        made = pltpu.make_async_copy(source, target, store.at[len(stores)])
        made.start()
        stores.append(made)

    barrier = pltpu.get_barrier_semaphore()
    always = [partner]
    if any(direct for _, _, direct in plan.segments):
        always += [chip_peer(k, n) for k, n in others]
    else:
        always += [pair_peer(k) for k in range(1, pairs)] + [lat_peer(k) for k in range(1, lats)]
    total = jnp.int32(len(always))
    for peer in always:
        pl.semaphore_signal(barrier, inc=1, device_id=peer, device_id_type=MESH)
    for s in (step - 1, step + 1):
        for l in (lat - 1, lat, lat + 1):
            there = present(s, l)

            @pl.when(there)
            def _(s=s, l=l):
                pl.semaphore_signal(barrier, inc=1, device_id={"step": s, "lat": l}, device_id_type=MESH)

            total = total + there.astype(jnp.int32)

    def place(wide, block):
        wide[HALO : HALO + rows] = jnp.swapaxes(block.astype(F32), 0, 1).astype(BF)

    def blank_edges(wide):
        @pl.when(jnp.logical_not(has_low))
        def _():
            wide[:HALO] = jnp.zeros((HALO, ch, width), BF)

        @pl.when(jnp.logical_not(has_high))
        def _():
            wide[HALO + rows :] = jnp.zeros((HALO, ch, width), BF)

    def remote(source, target, k, peer):
        return pltpu.make_async_remote_copy(
            src_ref=source, dst_ref=target, send_sem=send.at[k], recv_sem=recv.at[k],
            device_id=peer, device_id_type=MESH,
        )

    def halo(wide, k):
        up = remote(wide.at[pl.ds(rows, HALO)], wide.at[pl.ds(0, HALO)], k, {"lat": lat + 1})
        down = remote(wide.at[pl.ds(HALO, HALO)], wide.at[pl.ds(HALO + rows, HALO)], k + 1, {"lat": lat - 1})
        return up, down

    def start_halo(both, extra=None):
        up, down = both
        pl.when(has_high if extra is None else has_high & extra)(up.start)
        pl.when(has_low if extra is None else has_low & extra)(down.start)

    def wait_halo(both, extra=None):
        up, down = both
        low = has_low if extra is None else has_low & extra
        high = has_high if extra is None else has_high & extra
        pl.when(low)(up.wait_recv)
        pl.when(high)(down.wait_recv)
        pl.when(high)(up.wait_send)
        pl.when(low)(down.wait_send)

    def kept(value, row):
        g = lat * rows + (row - HALO)
        return jnp.where((g >= 0) & (g < rows * lats), value, 0.0)

    def halves(total):
        return total[:, :width], total[:, width:]

    def spread_rows(wide, dst, first, count, dilation, sign):
        each(count, lambda r: put_spread(dst, first + r, wide[first + r].astype(F32), dilation, sign))

    def conv1(v3, s1, h1, row):
        for k, part in enumerate(halves(dot(w1[...], row_pair(v3, row, (0, 1, 2))))):
            value, slope = gelu_pair(part)
            s1[row + k] = slope.astype(BF)
            put_spread(h1, row + k, kept(value, row + k + 1), 2, 1)

    def conv2(h1, h2, row):
        result = []
        for k, part in enumerate(halves(dot(w2[...], row_pair(h1, row, (0, 2, 4))))):
            value, slope = gelu_pair(part)
            h2[row + k] = kept(value, row + k + 3).astype(BF)
            result.append(slope)
        return result

    def conv3(x, h2, out, row):
        for k, part in enumerate(halves(dot(w3o[...], row_pair(h2, row, (0, 4, 8))))):
            out[row + k] = (x[row + k + HALO].astype(F32) + gathered(part, 4, 1)[:ch]).astype(BF)

    def back1(s1, row):
        for k, part in enumerate(halves(dot(w2b[...], row_pair(g2s, row, (4, 2, 0))))):
            delta = s1[row + k + 5].astype(F32) * part
            g1[row + k] = kept(delta, row + k + 6).astype(BF)

    def back0(cot, out, row):
        for k, part in enumerate(halves(dot(w1o[...], row_pair(g1, row, (2, 1, 0))))):
            out[row + k] = (cot[row + k + HALO].astype(F32) + gathered(part, 1, -1)[:ch]).astype(BF)

    def put_g2(row, delta):
        put_spread(g2s, row, kept(delta, row + 4), 2, -1)

    def last_term(h2, i):
        return nt(side(c3, 3 + (2 - i) * 4, rows, 0, 3 * cp), side(h2, 4, rows, 0, hid))

    def first_term(v3, i):
        return nt(side(v3, 6 + i, rows, 0, 3 * cp), side(g1, 1, rows, 0, hid))

    def mid_term(h1, i, j):
        return nt(side(h1, 6, rows, hid, 2 * hid), side(g2s, 1 + (2 - i) * 2, rows, j * hid, (j + 1) * hid))

    half_band = rows // 2

    def step_moves(block, target, distance, k):
        groups = []
        for group in (
            ((0, 0, half_band, HALO), (-1, 0, HALO, HALO + rows)),
            ((0, half_band, rows - half_band, HALO + half_band), (1, rows - HALO, HALO, 0)),
        ):
            moves = []
            for shift, source, count, into in group:
                made = remote(
                    block.at[pl.ds(source, count)], target.at[pl.ds(into, count)], k,
                    {"step": step + distance, "lat": lat + shift},
                )
                k += 1
                moves.append((present(step + distance, lat + shift), present(step - distance, lat - shift), into, count, made))
            groups.append(moves)
        return groups

    def start_moves(moves):
        for goes, comes, into, size, made in moves:
            pl.when(goes)(made.start)

    halo_state, halo_new, halo_late, halo_early = halo(xs, 0), halo(xl, 2), halo(cl, 4), halo(ce, 6)
    state_low, state_high = step_moves(out_e, xl, 1, 8)
    cot_low, cot_high = step_moves(adj_l, got, -1, 12)

    loads["state"].wait()
    place(xs, state[...])
    blank_edges(xs)
    pl.semaphore_wait(barrier, total)
    start_halo(halo_state)
    loads["new"].wait()
    pl.when(first_step)(lambda: place(xl, new[...]))
    start_halo(halo_new, first_step)
    blank_edges(xl)
    for wide in (v3e, v3l, c3):
        for j in range(3):
            wide[:, j * cp + ch : (j + 1) * cp, :] = jnp.zeros((ext, spare, width), BF)
    loads["kf"].wait()
    lay_out_across(kf, w1, spare)
    spread_rows(xs, v3e, HALO, rows, 1, 1)
    inner_first = HALO + 1
    inner_pairs = (rows - 4) // 2
    low_pairs = inner_first // 2
    high_first = inner_first + 2 * inner_pairs
    high_pairs = (rows + 12 - high_first) // 2
    half_pairs = half_band // 2
    each(inner_pairs, lambda c: conv1(v3e, s1e, h1e, inner_first + 2 * c))
    loads["km"].wait()
    lay_out_across(km, w2, 0)

    def early_conv2(row):
        for k, slope in enumerate(conv2(h1e, h2e, row)):
            s2e[row + k] = slope.astype(BF)

    each(inner_pairs - 2, lambda c: early_conv2(inner_first + 2 * c))
    loads["late"].wait()
    place(cl, late[...])
    blank_edges(cl)
    loads["early"].wait()
    place(ce, early[...])
    blank_edges(ce)
    loads["kl"].wait()
    lay_out_stacked(kl, w3o, spare)
    wait_halo(halo_state)
    start_halo(halo_late)
    spread_rows(xs, v3e, 0, HALO, 1, 1)
    each(low_pairs, lambda c: conv1(v3e, s1e, h1e, 2 * c))
    each(low_pairs, lambda c: early_conv2(2 * c))
    each(half_pairs, lambda c: conv3(xs, h2e, out_e, 2 * c))
    start_moves(state_low)
    spread_rows(xs, v3e, HALO + rows, HALO, 1, 1)
    each(high_pairs, lambda c: conv1(v3e, s1e, h1e, high_first + 2 * c))
    each(high_pairs, lambda c: early_conv2(high_first - 4 + 2 * c))
    each(half_pairs, lambda c: conv3(xs, h2e, out_e, half_band + 2 * c))
    start_moves(state_high)
    start_halo(halo_early)

    lay_out_across(kl, w3b, spare)
    lay_out_along(km, w2b)
    lay_out_stacked(kf, w1o, spare)
    wait_halo(halo_late)
    spread_rows(cl, c3, 0, ext, 4, -1)

    def late_back2(c):
        for k, part in enumerate(halves(dot(w3b[...], row_pair(c3, 2 * c, (8, 4, 0))))):
            b2[2 * c + k] = part

    each((rows + 6) // 2, late_back2)
    def late_conv2(row):
        for k, slope in enumerate(conv2(h1l, h2l, row)):
            r = row + k - 1
            put_g2(r, slope * b2[r])

    state_moves, cot_moves = state_low + state_high, cot_low + cot_high
    for goes, comes, into, size, made in (state_moves[0], state_moves[2]):
        pl.when(comes)(made.wait_recv)
    spread_rows(xl, v3l, HALO, rows, 1, 1)
    each(inner_pairs, lambda c: conv1(v3l, s1l, h1l, inner_first + 2 * c))
    each(inner_pairs - 2, lambda c: late_conv2(inner_first + 2 * c))
    wait_halo(halo_new, first_step)
    for goes, comes, into, size, made in state_moves[1:2]:
        pl.when(comes)(made.wait_recv)
    spread_rows(xl, v3l, HALO + rows, HALO, 1, 1)
    each(high_pairs, lambda c: conv1(v3l, s1l, h1l, high_first + 2 * c))
    each(high_pairs - 1, lambda c: late_conv2(high_first - 4 + 2 * c))
    conv2_last = conv2(h1l, h2l, rows + 6)
    put_g2(rows + 5, conv2_last[0] * b2[rows + 5])
    each(half_pairs + 1, lambda c: back1(s1l, half_band + 2 * c))
    each(half_pairs, lambda c: back0(cl, adj_l, half_band + 2 * c))
    start_moves(cot_high)
    for goes, comes, into, size, made in state_moves[3:]:
        pl.when(comes)(made.wait_recv)
    spread_rows(xl, v3l, 0, HALO, 1, 1)
    each(low_pairs, lambda c: conv1(v3l, s1l, h1l, 2 * c))
    conv2_first = conv2(h1l, h2l, 0)
    put_g2(0, conv2_first[1] * b2[0])
    each(low_pairs - 1, lambda c: late_conv2(2 * c + 2))
    each(half_pairs, lambda c: back1(s1l, 2 * c))
    each(half_pairs, lambda c: back0(cl, adj_l, 2 * c))
    start_moves(cot_low)

    @pl.loop(0, 3)
    def _(i):
        tl[i] = last_term(h2l, i)
        for j in range(3):
            tm[i, j] = mid_term(h1l, i, j)
        tf[i] = first_term(v3l, i)

    wait_halo(halo_early)
    def add_cot(moves):
        for goes, comes, into, size, made in moves:
            @pl.when(comes)
            def _(into=into, size=size, made=made):
                made.wait_recv()
                for r in range(into, into + size):
                    ce[r] = (ce[r].astype(F32) + got[r].astype(F32)).astype(BF)

    add_cot((cot_moves[0], cot_moves[2]))
    spread_rows(ce, c3, HALO, rows, 4, -1)
    add_cot((cot_moves[1], cot_moves[3]))
    spread_rows(ce, c3, 0, HALO, 4, -1)
    spread_rows(ce, c3, HALO + rows, HALO, 4, -1)

    slots = [0]

    def rows_at(start, size):
        return pl.ds(pl.multiple_of(start, 16), size)

    def copy(source, target, peer):
        slot = slots[0]
        slots[0] += 1
        made = pltpu.make_async_remote_copy(
            src_ref=source, dst_ref=target, send_sem=send_r.at[slot], recv_sem=recv_r.at[slot],
            device_id=peer, device_id_type=MESH,
        )
        made.start()
        return made

    def summing_direct(q):
        base, piece, _ = plan.segments[q]
        got_a, part, got_b = buffers[q]
        half = pairs * lats * piece
        mine_half = base + core * half
        me = pair * lats + lat
        made = copy(src.at[rows_at(base + (1 - core) * half, half)], got_a, partner)
        yield
        made.wait()
        part[...] = (src[rows_at(mine_half, half), :].astype(F32) + got_a[...].astype(F32)).astype(BF)
        flying = []
        for slot, (k, n) in enumerate(others):
            place_of = lax.rem(pair + k, pairs) * lats + lax.rem(lat + n, lats)
            flying.append(copy(part.at[rows_at(place_of * piece, piece)], got_b.at[slot], chip_peer(k, n)))
        yield
        for made in flying:
            made.wait()
        total = src[rows_at(mine_half + me * piece, piece), :].astype(F32)
        total = total + got_a[rows_at(me * piece, piece), :].astype(F32)
        for slot in range(len(others)):
            total = total + got_b[slot].astype(F32)
        mine = rows_at(mine_half + me * piece, piece)
        full[mine, :] = (total * scale).astype(BF)
        flying = [copy(full.at[mine], full.at[mine], chip_peer(k, n)) for k, n in others]
        yield
        for made in flying:
            made.wait()
        held = full.at[rows_at(mine_half, half)]
        made = copy(held, held, partner)
        yield
        made.wait()
        keep_segment(base, piece)
        yield

    def keep_segment(base, piece):
        whole = pl.ds(base, 2 * pairs * lats * piece)
        keep(full.at[whole], packed.at[whole])

    def summing(q):
        base, piece, direct = plan.segments[q]
        if direct:
            yield from summing_direct(q)
            return
        got_a, part_b, got_b, part_c, got_c = buffers[q]
        half, wedge = pairs * lats * piece, lats * piece
        mine_half = base + core * half
        flying = [copy(src.at[rows_at(base + (1 - core) * half, half)], got_a, partner)]

        def finish():
            for made in flying:
                made.wait()

        yield
        finish()
        part_b[...] = (src[rows_at(mine_half, half), :].astype(F32) + got_a[...].astype(F32)).astype(BF)
        flying = [
            copy(part_b.at[rows_at(lax.rem(pair + k, pairs) * wedge, wedge)], got_b.at[k - 1], pair_peer(k))
            for k in range(1, pairs)
        ]
        yield
        finish()
        total = src[rows_at(mine_half + pair * wedge, wedge), :].astype(F32)
        total = total + got_a[rows_at(pair * wedge, wedge), :].astype(F32)
        for k in range(pairs - 1):
            total = total + got_b[k].astype(F32)
        part_c[...] = total.astype(BF)
        flying = [
            copy(part_c.at[rows_at(lax.rem(lat + k, lats) * piece, piece)], got_c.at[k - 1], lat_peer(k))
            for k in range(1, lats)
        ]
        yield
        finish()
        total = part_c[rows_at(lat * piece, piece), :].astype(F32)
        for k in range(lats - 1):
            total = total + got_c[k].astype(F32)
        mine = rows_at(mine_half + pair * wedge + lat * piece, piece)
        full[mine, :] = (total * scale).astype(BF)
        flying = [copy(full.at[mine], full.at[mine], lat_peer(k)) for k in range(1, lats)]
        yield
        finish()
        held = full.at[rows_at(mine_half + pair * wedge, wedge)]
        flying = [copy(held, held, pair_peer(k)) for k in range(1, pairs)]
        yield
        finish()
        held = full.at[rows_at(mine_half, half)]
        flying = [copy(held, held, partner)]
        yield
        finish()
        keep_segment(base, piece)
        yield

    def blocks_of(terms):
        return [terms[i, j * cp : j * cp + ch] for i in range(3) for j in range(3)]

    lane = plan.lane

    sums = [summing(q) for q in range(len(plan.segments))]
    sum_last, sum_mids, sum_first = sums[0], sums[1:-1], sums[-1]

    def advance(*which):
        for one in which:
            next(one, None)

    def early_back2(c):
        for k, part in enumerate(halves(dot(w3b[...], row_pair(c3, 2 * c, (8, 4, 0))))):
            row = 2 * c + k
            put_g2(row, s2e[row + 1].astype(F32) * part)

    each((rows + 6) // 2, early_back2)
    tap = 0
    for k, ready in enumerate(plan.taps_ready):
        for t in range(tap, ready):
            value = tm[t // 3, t % 3] + mid_term(h1e, t // 3, t % 3)
            start = plan.mid + t * plan.mid_tap
            src[start : start + plan.mid_tap, :] = pack_terms([value], lane, plan.mid_tap)
        tap = ready
        if tap == 9 and plan.gap[1] > plan.gap[0]:
            src[plan.gap[0] : plan.gap[1], :] = jnp.zeros((plan.gap[1] - plan.gap[0], lane), BF)
        advance(sum_mids[k])
        if k == 1:
            advance(sum_mids[0])

    @pl.loop(0, 3, unroll=3)
    def _(i):
        tl[i] = tl[i] + last_term(h2e, i)

    src[: plan.mid, :] = pack_terms(blocks_of(tl), lane, plan.mid)
    advance(sum_last, *sum_mids[1:])
    each((rows + 2) // 2, lambda c: back1(s1e, 2 * c))
    advance(sum_last)

    @pl.loop(0, 3, unroll=3)
    def _(i):
        tf[i] = tf[i] + first_term(v3e, i)

    src[plan.first :, :] = pack_terms(blocks_of(tf), lane, plan.rows - plan.first)
    advance(sum_first, sum_mids[0])
    each(rows // 2, lambda c: back0(ce, adj, 2 * c))
    keep(adj, adj_out)
    advance(sum_first, *sum_mids[1:])
    each(rows // 2, lambda c: conv3(xl, h2l, adv, 2 * c))
    keep(adv, adv_out)
    advance(sum_mids[0], sum_last, *sum_mids[1:])
    advance(sum_first, *sum_mids)
    advance(sum_last, sum_mids[0], sum_first, *sum_mids[1:])
    for _ in range(7):
        advance(sum_last, *sum_mids, sum_first)

    for goes, comes, into, size, made in state_moves + cot_moves:
        pl.when(goes)(made.wait_send)
    for made in stores:
        made.wait()


def unpack_kernel(
    plan, adv_in, adj_in, packed_in, adv_out, adj_out, first_out, mid_out, last_out,
    adv, adj, packed, out_adv, out_adj, out_first, out_mid, out_last, load, store,
):
    taps, ch, hid = out_first.shape
    lane = plan.lane
    rest = hid - lane
    small = pl.ds(plan.last, plan.small)
    mids = pl.ds(plan.mid, taps * plan.mid_tap)
    firsts = pl.ds(plan.first, plan.small)
    loads = [
        pltpu.make_async_copy(source, target, load.at[n])
        for n, (source, target) in enumerate((
            (packed_in.at[mids], packed.at[mids]), (packed_in.at[small], packed.at[small]),
            (packed_in.at[firsts], packed.at[firsts]), (adv_in, adv), (adj_in, adj),
        ))
    ]
    for made in loads:
        made.start()
    stores = []

    def keep(source, target):
        made = pltpu.make_async_copy(source, target, store.at[len(stores)])
        made.start()
        stores.append(made)

    loads[0].wait()
    cut = half_rows(hid)
    for group in range(3):
        for t in range(3 * group, 3 * group + 3):
            start = plan.mid + t * plan.mid_tap
            value = packed[start : start + plan.mid_tap, :].astype(F32)
            out_mid[t, :, :lane] = value[:hid]
            out_mid[t, :cut, lane:] = value[hid : hid + cut, :rest]
            out_mid[t, cut:, lane:] = value[hid : hid + cut, rest:]
        part = pl.ds(3 * group, 3)
        keep(out_mid.at[part], mid_out.at[part])
    for made, start, out, target in (
        (loads[1], plan.last, out_last, last_out), (loads[2], plan.first, out_first, first_out)
    ):
        made.wait()
        count = taps * ch
        cut = half_rows(count)
        value = packed[start : start + plan.small, :].astype(F32)
        tails = value[count : count + cut]
        tails = jnp.concatenate([tails[:, :rest], tails[:, rest:]], axis=0)
        for t in range(taps):
            out[t, :, :lane] = value[t * ch : (t + 1) * ch]
            out[t, :, lane:] = tails[t * ch : (t + 1) * ch]
        keep(out, target)
    for made, source, out, target in ((loads[3], adv, out_adv, adv_out), (loads[4], adj, out_adj, adj_out)):
        made.wait()
        out[...] = jnp.swapaxes(source[...].astype(F32), 0, 1).astype(BF)
        keep(out, target.at[0])
    for made in stores:
        made.wait()


def body(state_in, new_state, cot_early, cot_late, kernel_first, kernel_mid, kernel_last):
    steps, lats = lax.axis_size("step"), lax.axis_size("lat")
    ch, rows, width = new_state.shape
    hid = kernel_mid.shape[1]
    taps = kernel_mid.shape[0]
    cp = -(-ch // 16) * 16
    plan = Plan(steps, lats, ch, hid)
    lane = plan.lane
    scale = 1.0 / math.sqrt(2.0 * steps * rows * lats * width)

    vmem = pl.BlockSpec(memory_space=pltpu.VMEM)
    shape = jax.ShapeDtypeStruct
    ext, ext_1, ext_2 = rows + 14, rows + 12, rows + 8
    band_in = ((ch, rows, width), BF)
    moved = [band_in] * 4 + [
        ((taps, ch, hid), BF), ((taps, hid, hid), BF), ((taps, ch, hid), BF),
        ((rows, ch, width), BF), ((rows, ch, width), BF), ((plan.rows, lane), BF),
    ]
    scratch = [((ext, ch, width), BF)] * 5 + [
        ((hid, 9 * cp), BF), ((hid, 9 * hid), BF), ((3 * cp, 3 * hid), BF),
        ((3 * cp, 3 * hid), BF), ((hid, 9 * hid), BF), ((hid, 9 * cp), BF),
        ((ext, 3 * cp, width), BF), ((ext, 3 * cp, width), BF),
        ((ext_1, 3 * hid, width), BF), ((ext_1, 3 * hid, width), BF),
        ((ext_2, hid, width), BF), ((ext_2, hid, width), BF),
        ((ext_1, hid, width), BF), ((ext_1, hid, width), BF),
        ((ext_2, hid, width), BF),
        ((ext, 3 * cp, width), BF), ((rows + 6, 3 * hid, width), BF), ((rows + 2, hid, width), BF),
        ((rows + 6, hid, width), F32),
        ((rows, ch, width), BF), ((rows, ch, width), BF),
        ((3, 3 * cp, hid), F32), ((3, 3, hid, hid), F32), ((3, 3 * cp, hid), F32),
        ((plan.rows, lane), BF),
    ]
    for dims in plan.shapes:
        scratch += [(d + (lane,), BF) for d in dims]
    sems = pltpu.SemaphoreType.DMA
    band_shape = shape((rows, ch, width), BF)
    anywhere = pl.BlockSpec(memory_space=pl.ANY)
    advanced, adjoint, packed = pl.pallas_call(
        functools.partial(mega_kernel, rows, width, steps, lats, scale, plan),
        out_shape=[band_shape, band_shape, shape((plan.rows, lane), BF)],
        in_specs=[anywhere] * 7,
        out_specs=[anywhere] * 3,
        scratch_shapes=[pltpu.VMEM(*s) for s in moved] + [
            sems((7,)), sems((2 + len(plan.segments),)),
        ] + [pltpu.VMEM(*s) for s in scratch] + [sems((16,)), sems((16,)), sems((plan.slots,)), sems((plan.slots,))],
        compiler_params=pltpu.CompilerParams(
            collective_id=0, has_side_effects=True, vmem_limit_bytes=60 * 1024 * 1024
        ),
        name="rollout",
    )(state_in, new_state, cot_late, cot_early, kernel_first, kernel_mid, kernel_last)
    return pl.pallas_call(
        functools.partial(unpack_kernel, plan),
        out_shape=[
            shape((1, ch, rows, width), BF), shape((1, ch, rows, width), BF),
            shape((taps, ch, hid), F32), shape((taps, hid, hid), F32), shape((taps, ch, hid), F32),
        ],
        in_specs=[anywhere] * 3,
        out_specs=[anywhere] * 5,
        scratch_shapes=[
            pltpu.VMEM(*s) for s in moved[7:] + [band_in, band_in] + [
                ((taps, ch, hid), F32), ((taps, hid, hid), F32), ((taps, ch, hid), F32),
            ]
        ] + [sems((5,)), sems((7,))],
        compiler_params=pltpu.CompilerParams(vmem_limit_bytes=60 * 1024 * 1024),
        name="unpack_terms",
    )(advanced, adjoint, packed)


def solution(mesh):
    banded = P("step", None, "lat", None)
    return jax.shard_map(
        body,
        mesh=mesh,
        in_specs=(banded, P(None, "lat", None), banded, banded, P(), P(), P()),
        out_specs=(banded, banded, P(), P(), P()),
        check_vma=False,
    )
```

```python
import functools
import math

import jax
import jax.numpy as jnp
from jax import lax
from jax.experimental import pallas as pl
from jax.experimental.pallas import tpu as pltpu
from jax.sharding import PartitionSpec as P

MESH = pl.DeviceIdType.MESH
BF = jnp.bfloat16
F32 = jnp.float32
HALO = 7
NT = (((1,), (1,)), ((), ()))


def gelu_pair(a):
    c0 = math.sqrt(2.0 / math.pi)
    c1 = c0 * 0.044715
    sq = a * a
    t = jnp.tanh(a * (c0 + c1 * sq))
    half = 0.5 + 0.5 * t
    slope = half + (a * (1.0 - t * t)) * (0.5 * c0 + (1.5 * c1) * sq)
    return a * half, slope


def row_pair(src, row, offsets):
    return jnp.concatenate(
        [jnp.concatenate([src[row + k + o] for o in offsets], axis=0) for k in range(2)], axis=1
    )


def shifted(value, shift):
    width = value.shape[1]
    if shift == 0:
        return value
    column = lax.broadcasted_iota(jnp.int32, value.shape, 1)
    moved = pltpu.roll(value, (-shift) % width, 1)
    good = (column < width - shift) if shift > 0 else (column >= -shift)
    return jnp.where(good, moved, 0.0)


def put_spread(dst, row, value, dilation, sign):
    channels, pitch = value.shape[0], dst.shape[1] // 3
    for j in range(3):
        dst[row, j * pitch : j * pitch + channels, :] = shifted(value, sign * dilation * (j - 1)).astype(BF)


def gathered(total, dilation, sign):
    channels = total.shape[0] // 3
    acc = total[channels : 2 * channels]
    for j in (0, 2):
        acc = acc + shifted(total[j * channels : (j + 1) * channels], sign * dilation * (j - 1))
    return acc


def each(count, work, unroll=None):
    pl.loop(0, count, unroll=count if unroll is None else unroll)(work)


def dot(a, b):
    return jnp.dot(a, b, preferred_element_type=F32)


def nt(a, b):
    return lax.dot_general(a, b, NT, preferred_element_type=F32)


def side(src, row, count, low, high):
    return jnp.concatenate([src[row + k, low:high] for k in range(count)], axis=1)


def tall(kernel, spare):
    taps, _, hid = kernel.shape
    block = [kernel[t].astype(F32) for t in range(taps)]
    if spare:
        block = [jnp.concatenate([b, jnp.zeros((spare, hid), F32)], axis=0) for b in block]
    return block


def lay_out_across(kernel, out, spare):
    out[...] = jnp.transpose(jnp.concatenate(tall(kernel, spare), axis=0)).astype(BF)


def lay_out_along(kernel, out):
    out[...] = jnp.concatenate(tall(kernel, 0), axis=1).astype(BF)


def lay_out_stacked(kernel, out, spare):
    blocks = tall(kernel, spare)
    size = blocks[0].shape[0]
    for j in range(3):
        out[j * size : (j + 1) * size, :] = jnp.concatenate(
            [blocks[3 * i + j] for i in range(3)], axis=1
        ).astype(BF)


def pack_terms(blocks, lane, size):
    rest = blocks[0].shape[1] - lane
    main = jnp.concatenate([b[:, :lane] for b in blocks], axis=0)
    tails = jnp.concatenate([b[:, lane:] for b in blocks], axis=0)
    count = main.shape[0]
    cut = half_rows(count)
    low = tails[cut:]
    if cut * 2 > count:
        low = jnp.concatenate([low, jnp.zeros((2 * cut - count, rest), F32)], axis=0)
    parts = [main, jnp.concatenate([tails[:cut], low], axis=1)]
    if size > count + cut:
        parts.append(jnp.zeros((size - count - cut, lane), F32))
    return jnp.concatenate(parts, axis=0).astype(BF)


def half_rows(count):
    return -(-count // 16) * 8


class Plan:
    def __init__(self, steps, lats, ch, hid):
        devices = steps * lats
        unit = 16 * devices
        self.lane = 128
        taps = 9
        small = taps * ch + half_rows(taps * ch)
        self.mid_tap = hid + hid // 2
        mid = taps * self.mid_tap
        self.small = -(-small // 16) * 16
        self.mid, self.last = 0, mid
        units = -(-(mid + self.small) // unit)
        sizes = [2, 2, units - 4] if units >= 5 else [1, units - 1] if units >= 2 else [units]
        edge = 0
        self.segments, self.taps_ready = [], []
        for size in sizes:
            self.segments.append((edge, 16 * size))
            edge += size * unit
            self.taps_ready.append(min(taps, -(-edge // self.mid_tap)))
        self.taps_ready[-1] = taps
        self.first = edge
        first_units = -(-self.small // unit)
        self.segments.append((edge, 16 * first_units))
        self.gap = (self.last + self.small, self.first)
        self.rows = edge + first_units * unit
        chips = devices // 2
        pairs = steps // 2
        self.shapes, self.slots = [], 0
        for _, piece in self.segments:
            half, wedge = chips * piece, lats * piece
            self.shapes.append([
                (half,), (half,), (max(pairs - 1, 1), wedge), (wedge,), (max(lats - 1, 1), piece),
            ])
            self.slots += 2 + 2 * (pairs - 1) + 2 * (lats - 1)


def mega_kernel(
    rows, width, steps, lats, scale, plan,
    state_in, new_in, late_in, early_in, kf_in, km_in, kl_in,
    adv_out, adj_out, packed,
    state, new, late, early, kf, km, kl, adv, adj, full, load, store,
    xs, xl, cl, ce, got, w1, w2, w3o, w1o, w2b, w3b,
    v3e, v3l, h1e, h1l, h2e, h2l, s1e, s1l, s2e, c3, g2s, g1, b2, out_e, adj_l,
    tf, tm, tl, src, *rest,
):
    buffers = []
    for dims in plan.shapes:
        buffers.append(rest[: len(dims)])
        rest = rest[len(dims) :]
    send, recv, send_r, recv_r = rest
    lat = lax.axis_index("lat")
    step = lax.axis_index("step")
    ch = xs.shape[1]
    cp, hid = c3.shape[1] // 3, w2.shape[0]
    spare = cp - ch
    ext = rows + 2 * HALO
    pairs = steps // 2
    core = lax.rem(step, 2)
    pair = step // 2
    has_low, has_high = lat > 0, lat < lats - 1
    first_step = step == 0

    def present(s, l):
        return (s >= 0) & (s < steps) & (l >= 0) & (l < lats)

    partner = {"step": pair * 2 + (1 - core)}

    def pair_peer(k):
        return {"step": lax.rem(pair + k, pairs) * 2 + core}

    def lat_peer(k):
        return {"lat": lax.rem(lat + k, lats)}

    loads = {}
    for n, (name, source, target) in enumerate((
        ("state", state_in.at[0], state), ("kf", kf_in, kf), ("new", new_in, new), ("km", km_in, km),
        ("late", late_in.at[0], late), ("early", early_in.at[0], early), ("kl", kl_in, kl),
    )):
        loads[name] = pltpu.make_async_copy(source, target, load.at[n])
        loads[name].start()
    stores = []

    def keep(source, target):
        made = pltpu.make_async_copy(source, target, store.at[len(stores)])
        made.start()
        stores.append(made)

    barrier = pltpu.get_barrier_semaphore()
    always = [partner] + [pair_peer(k) for k in range(1, pairs)] + [lat_peer(k) for k in range(1, lats)]
    total = jnp.int32(len(always))
    for peer in always:
        pl.semaphore_signal(barrier, inc=1, device_id=peer, device_id_type=MESH)
    for s in (step - 1, step + 1):
        for l in (lat - 1, lat, lat + 1):
            there = present(s, l)

            @pl.when(there)
            def _(s=s, l=l):
                pl.semaphore_signal(barrier, inc=1, device_id={"step": s, "lat": l}, device_id_type=MESH)

            total = total + there.astype(jnp.int32)

    def place(wide, block):
        wide[HALO : HALO + rows] = jnp.swapaxes(block.astype(F32), 0, 1).astype(BF)

    def blank_edges(wide):
        @pl.when(jnp.logical_not(has_low))
        def _():
            wide[:HALO] = jnp.zeros((HALO, ch, width), BF)

        @pl.when(jnp.logical_not(has_high))
        def _():
            wide[HALO + rows :] = jnp.zeros((HALO, ch, width), BF)

    def remote(source, target, k, peer):
        return pltpu.make_async_remote_copy(
            src_ref=source, dst_ref=target, send_sem=send.at[k], recv_sem=recv.at[k],
            device_id=peer, device_id_type=MESH,
        )

    def halo(wide, k):
        up = remote(wide.at[pl.ds(rows, HALO)], wide.at[pl.ds(0, HALO)], k, {"lat": lat + 1})
        down = remote(wide.at[pl.ds(HALO, HALO)], wide.at[pl.ds(HALO + rows, HALO)], k + 1, {"lat": lat - 1})
        return up, down

    def start_halo(both, extra=None):
        up, down = both
        pl.when(has_high if extra is None else has_high & extra)(up.start)
        pl.when(has_low if extra is None else has_low & extra)(down.start)

    def wait_halo(both, extra=None):
        up, down = both
        low = has_low if extra is None else has_low & extra
        high = has_high if extra is None else has_high & extra
        pl.when(low)(up.wait_recv)
        pl.when(high)(down.wait_recv)
        pl.when(high)(up.wait_send)
        pl.when(low)(down.wait_send)

    def kept(value, row):
        g = lat * rows + (row - HALO)
        return jnp.where((g >= 0) & (g < rows * lats), value, 0.0)

    def halves(total):
        return total[:, :width], total[:, width:]

    def spread_rows(wide, dst, first, count, dilation, sign):
        each(count, lambda r: put_spread(dst, first + r, wide[first + r].astype(F32), dilation, sign))

    def conv1(v3, s1, h1, row):
        for k, part in enumerate(halves(dot(w1[...], row_pair(v3, row, (0, 1, 2))))):
            value, slope = gelu_pair(part)
            s1[row + k] = slope.astype(BF)
            put_spread(h1, row + k, kept(value, row + k + 1), 2, 1)

    def conv2(h1, h2, row):
        result = []
        for k, part in enumerate(halves(dot(w2[...], row_pair(h1, row, (0, 2, 4))))):
            value, slope = gelu_pair(part)
            h2[row + k] = kept(value, row + k + 3).astype(BF)
            result.append(slope)
        return result

    def conv3(x, h2, out, row):
        for k, part in enumerate(halves(dot(w3o[...], row_pair(h2, row, (0, 4, 8))))):
            out[row + k] = (x[row + k + HALO].astype(F32) + gathered(part, 4, 1)[:ch]).astype(BF)

    def back1(s1, row):
        for k, part in enumerate(halves(dot(w2b[...], row_pair(g2s, row, (4, 2, 0))))):
            delta = s1[row + k + 5].astype(F32) * part
            g1[row + k] = kept(delta, row + k + 6).astype(BF)

    def back0(cot, out, row):
        for k, part in enumerate(halves(dot(w1o[...], row_pair(g1, row, (2, 1, 0))))):
            out[row + k] = (cot[row + k + HALO].astype(F32) + gathered(part, 1, -1)[:ch]).astype(BF)

    def put_g2(row, delta):
        put_spread(g2s, row, kept(delta, row + 4), 2, -1)

    def last_term(h2, i):
        return nt(side(c3, 3 + (2 - i) * 4, rows, 0, 3 * cp), side(h2, 4, rows, 0, hid))

    def first_term(v3, i):
        return nt(side(v3, 6 + i, rows, 0, 3 * cp), side(g1, 1, rows, 0, hid))

    def mid_term(h1, i, j):
        return nt(side(h1, 6, rows, hid, 2 * hid), side(g2s, 1 + (2 - i) * 2, rows, j * hid, (j + 1) * hid))

    half_band = rows // 2

    def step_moves(block, target, distance, k):
        groups = []
        for group in (
            ((0, 0, half_band, HALO), (-1, 0, HALO, HALO + rows)),
            ((0, half_band, rows - half_band, HALO + half_band), (1, rows - HALO, HALO, 0)),
        ):
            moves = []
            for shift, source, count, into in group:
                made = remote(
                    block.at[pl.ds(source, count)], target.at[pl.ds(into, count)], k,
                    {"step": step + distance, "lat": lat + shift},
                )
                k += 1
                moves.append((present(step + distance, lat + shift), present(step - distance, lat - shift), into, count, made))
            groups.append(moves)
        return groups

    def start_moves(moves):
        for goes, comes, into, size, made in moves:
            pl.when(goes)(made.start)

    halo_state, halo_new, halo_late, halo_early = halo(xs, 0), halo(xl, 2), halo(cl, 4), halo(ce, 6)
    state_low, state_high = step_moves(out_e, xl, 1, 8)
    cot_low, cot_high = step_moves(adj_l, got, -1, 12)

    loads["state"].wait()
    place(xs, state[...])
    blank_edges(xs)
    pl.semaphore_wait(barrier, total)
    start_halo(halo_state)
    loads["new"].wait()
    pl.when(first_step)(lambda: place(xl, new[...]))
    start_halo(halo_new, first_step)
    blank_edges(xl)
    for wide in (v3e, v3l, c3):
        for j in range(3):
            wide[:, j * cp + ch : (j + 1) * cp, :] = jnp.zeros((ext, spare, width), BF)
    loads["kf"].wait()
    lay_out_across(kf, w1, spare)
    spread_rows(xs, v3e, HALO, rows, 1, 1)
    inner_first = HALO + 1
    inner_pairs = (rows - 4) // 2
    low_pairs = inner_first // 2
    high_first = inner_first + 2 * inner_pairs
    high_pairs = (rows + 12 - high_first) // 2
    half_pairs = half_band // 2
    each(inner_pairs, lambda c: conv1(v3e, s1e, h1e, inner_first + 2 * c))
    loads["km"].wait()
    lay_out_across(km, w2, 0)

    def early_conv2(row):
        for k, slope in enumerate(conv2(h1e, h2e, row)):
            s2e[row + k] = slope.astype(BF)

    each(inner_pairs - 2, lambda c: early_conv2(inner_first + 2 * c))
    loads["late"].wait()
    place(cl, late[...])
    blank_edges(cl)
    loads["early"].wait()
    place(ce, early[...])
    blank_edges(ce)
    loads["kl"].wait()
    lay_out_stacked(kl, w3o, spare)
    wait_halo(halo_state)
    start_halo(halo_late)
    spread_rows(xs, v3e, 0, HALO, 1, 1)
    each(low_pairs, lambda c: conv1(v3e, s1e, h1e, 2 * c))
    each(low_pairs, lambda c: early_conv2(2 * c))
    each(half_pairs, lambda c: conv3(xs, h2e, out_e, 2 * c))
    start_moves(state_low)
    spread_rows(xs, v3e, HALO + rows, HALO, 1, 1)
    each(high_pairs, lambda c: conv1(v3e, s1e, h1e, high_first + 2 * c))
    each(high_pairs, lambda c: early_conv2(high_first - 4 + 2 * c))
    each(half_pairs, lambda c: conv3(xs, h2e, out_e, half_band + 2 * c))
    start_moves(state_high)
    start_halo(halo_early)

    lay_out_across(kl, w3b, spare)
    lay_out_along(km, w2b)
    lay_out_stacked(kf, w1o, spare)
    wait_halo(halo_late)
    spread_rows(cl, c3, 0, ext, 4, -1)

    def late_back2(c):
        for k, part in enumerate(halves(dot(w3b[...], row_pair(c3, 2 * c, (8, 4, 0))))):
            b2[2 * c + k] = part

    each((rows + 6) // 2, late_back2)
    def late_conv2(row):
        for k, slope in enumerate(conv2(h1l, h2l, row)):
            r = row + k - 1
            put_g2(r, slope * b2[r])

    state_moves, cot_moves = state_low + state_high, cot_low + cot_high
    for goes, comes, into, size, made in (state_moves[0], state_moves[2]):
        pl.when(comes)(made.wait_recv)
    spread_rows(xl, v3l, HALO, rows, 1, 1)
    each(inner_pairs, lambda c: conv1(v3l, s1l, h1l, inner_first + 2 * c))
    each(inner_pairs - 2, lambda c: late_conv2(inner_first + 2 * c))
    wait_halo(halo_new, first_step)
    for goes, comes, into, size, made in state_moves[1:2]:
        pl.when(comes)(made.wait_recv)
    spread_rows(xl, v3l, HALO + rows, HALO, 1, 1)
    each(high_pairs, lambda c: conv1(v3l, s1l, h1l, high_first + 2 * c))
    each(high_pairs - 1, lambda c: late_conv2(high_first - 4 + 2 * c))
    conv2_last = conv2(h1l, h2l, rows + 6)
    put_g2(rows + 5, conv2_last[0] * b2[rows + 5])
    each(half_pairs + 1, lambda c: back1(s1l, half_band + 2 * c))
    each(half_pairs, lambda c: back0(cl, adj_l, half_band + 2 * c))
    start_moves(cot_high)
    for goes, comes, into, size, made in state_moves[3:]:
        pl.when(comes)(made.wait_recv)
    spread_rows(xl, v3l, 0, HALO, 1, 1)
    each(low_pairs, lambda c: conv1(v3l, s1l, h1l, 2 * c))
    conv2_first = conv2(h1l, h2l, 0)
    put_g2(0, conv2_first[1] * b2[0])
    each(low_pairs - 1, lambda c: late_conv2(2 * c + 2))
    each(half_pairs, lambda c: back1(s1l, 2 * c))
    each(half_pairs, lambda c: back0(cl, adj_l, 2 * c))
    start_moves(cot_low)

    @pl.loop(0, 3)
    def _(i):
        tl[i] = last_term(h2l, i)
        for j in range(3):
            tm[i, j] = mid_term(h1l, i, j)
        tf[i] = first_term(v3l, i)

    wait_halo(halo_early)
    def add_cot(moves):
        for goes, comes, into, size, made in moves:
            @pl.when(comes)
            def _(into=into, size=size, made=made):
                made.wait_recv()
                for r in range(into, into + size):
                    ce[r] = (ce[r].astype(F32) + got[r].astype(F32)).astype(BF)

    add_cot((cot_moves[0], cot_moves[2]))
    spread_rows(ce, c3, HALO, rows, 4, -1)
    add_cot((cot_moves[1], cot_moves[3]))
    spread_rows(ce, c3, 0, HALO, 4, -1)
    spread_rows(ce, c3, HALO + rows, HALO, 4, -1)

    slots = [0]

    def rows_at(start, size):
        return pl.ds(pl.multiple_of(start, 16), size)

    def copy(source, target, peer):
        slot = slots[0]
        slots[0] += 1
        made = pltpu.make_async_remote_copy(
            src_ref=source, dst_ref=target, send_sem=send_r.at[slot], recv_sem=recv_r.at[slot],
            device_id=peer, device_id_type=MESH,
        )
        made.start()
        return made

    def keep_segment(base, piece):
        whole = pl.ds(base, 2 * pairs * lats * piece)
        keep(full.at[whole], packed.at[whole])

    def summing(q):
        base, piece = plan.segments[q]
        got_a, part_b, got_b, part_c, got_c = buffers[q]
        half, wedge = pairs * lats * piece, lats * piece
        mine_half = base + core * half
        flying = [copy(src.at[rows_at(base + (1 - core) * half, half)], got_a, partner)]

        def finish():
            for made in flying:
                made.wait()

        yield
        finish()
        part_b[...] = (src[rows_at(mine_half, half), :].astype(F32) + got_a[...].astype(F32)).astype(BF)
        flying = [
            copy(part_b.at[rows_at(lax.rem(pair + k, pairs) * wedge, wedge)], got_b.at[k - 1], pair_peer(k))
            for k in range(1, pairs)
        ]
        yield
        finish()
        total = src[rows_at(mine_half + pair * wedge, wedge), :].astype(F32)
        total = total + got_a[rows_at(pair * wedge, wedge), :].astype(F32)
        for k in range(pairs - 1):
            total = total + got_b[k].astype(F32)
        part_c[...] = total.astype(BF)
        flying = [
            copy(part_c.at[rows_at(lax.rem(lat + k, lats) * piece, piece)], got_c.at[k - 1], lat_peer(k))
            for k in range(1, lats)
        ]
        yield
        finish()
        total = part_c[rows_at(lat * piece, piece), :].astype(F32)
        for k in range(lats - 1):
            total = total + got_c[k].astype(F32)
        mine = rows_at(mine_half + pair * wedge + lat * piece, piece)
        full[mine, :] = (total * scale).astype(BF)
        flying = [copy(full.at[mine], full.at[mine], lat_peer(k)) for k in range(1, lats)]
        yield
        finish()
        held = full.at[rows_at(mine_half + pair * wedge, wedge)]
        flying = [copy(held, held, pair_peer(k)) for k in range(1, pairs)]
        yield
        finish()
        held = full.at[rows_at(mine_half, half)]
        flying = [copy(held, held, partner)]
        yield
        finish()
        keep_segment(base, piece)
        yield

    def blocks_of(terms):
        return [terms[i, j * cp : j * cp + ch] for i in range(3) for j in range(3)]

    lane = plan.lane

    sums = [summing(q) for q in range(len(plan.segments))]
    early_sums, sum_last, sum_first = sums[:-2], sums[-2], sums[-1]

    def advance(*which):
        for one in which:
            next(one, None)

    def early_back2(c):
        for k, part in enumerate(halves(dot(w3b[...], row_pair(c3, 2 * c, (8, 4, 0))))):
            row = 2 * c + k
            put_g2(row, s2e[row + 1].astype(F32) * part)

    each((rows + 6) // 2, early_back2)
    tap = 0
    for k, ready in enumerate(plan.taps_ready):
        for t in range(tap, ready):
            value = tm[t // 3, t % 3] + mid_term(h1e, t // 3, t % 3)
            start = plan.mid + t * plan.mid_tap
            src[start : start + plan.mid_tap, :] = pack_terms([value], lane, plan.mid_tap)
        tap = ready
        if k < len(early_sums):
            advance(*early_sums[: k + 1][::-1])

    @pl.loop(0, 3, unroll=3)
    def _(i):
        tl[i] = tl[i] + last_term(h2e, i)

    src[plan.last : plan.last + plan.small, :] = pack_terms(blocks_of(tl), lane, plan.small)
    if plan.gap[1] > plan.gap[0]:
        src[plan.gap[0] : plan.gap[1], :] = jnp.zeros((plan.gap[1] - plan.gap[0], lane), BF)
    advance(sum_last, *early_sums[1:])
    each((rows + 2) // 2, lambda c: back1(s1e, 2 * c))
    advance(sum_last)

    @pl.loop(0, 3, unroll=3)
    def _(i):
        tf[i] = tf[i] + first_term(v3e, i)

    src[plan.first :, :] = pack_terms(blocks_of(tf), lane, plan.rows - plan.first)
    advance(sum_first, *early_sums[:1])
    each(rows // 2, lambda c: back0(ce, adj, 2 * c))
    keep(adj, adj_out)
    advance(sum_first, *early_sums[1:])
    each(rows // 2, lambda c: conv3(xl, h2l, adv, 2 * c))
    keep(adv, adv_out)
    for _ in range(7):
        advance(sum_last, *early_sums, sum_first)

    for goes, comes, into, size, made in state_moves + cot_moves:
        pl.when(goes)(made.wait_send)
    for made in stores:
        made.wait()


def unpack_kernel(
    plan, adv_in, adj_in, packed_in, adv_out, adj_out, first_out, mid_out, last_out,
    adv, adj, packed, out_adv, out_adj, out_first, out_mid, out_last, load, store,
):
    taps, ch, hid = out_first.shape
    lane = plan.lane
    rest = hid - lane
    small = pl.ds(plan.last, plan.small)
    mids = pl.ds(plan.mid, taps * plan.mid_tap)
    firsts = pl.ds(plan.first, plan.small)
    loads = [
        pltpu.make_async_copy(source, target, load.at[n])
        for n, (source, target) in enumerate((
            (packed_in.at[mids], packed.at[mids]), (packed_in.at[small], packed.at[small]),
            (packed_in.at[firsts], packed.at[firsts]), (adv_in, adv), (adj_in, adj),
        ))
    ]
    for made in loads:
        made.start()
    stores = []

    def keep(source, target):
        made = pltpu.make_async_copy(source, target, store.at[len(stores)])
        made.start()
        stores.append(made)

    loads[0].wait()
    cut = half_rows(hid)
    for group in range(3):
        for t in range(3 * group, 3 * group + 3):
            start = plan.mid + t * plan.mid_tap
            value = packed[start : start + plan.mid_tap, :].astype(F32)
            out_mid[t, :, :lane] = value[:hid]
            out_mid[t, :cut, lane:] = value[hid : hid + cut, :rest]
            out_mid[t, cut:, lane:] = value[hid : hid + cut, rest:]
        part = pl.ds(3 * group, 3)
        keep(out_mid.at[part], mid_out.at[part])
    for made, start, out, target in (
        (loads[1], plan.last, out_last, last_out), (loads[2], plan.first, out_first, first_out)
    ):
        made.wait()
        count = taps * ch
        cut = half_rows(count)
        value = packed[start : start + plan.small, :].astype(F32)
        tails = value[count : count + cut]
        tails = jnp.concatenate([tails[:, :rest], tails[:, rest:]], axis=0)
        for t in range(taps):
            out[t, :, :lane] = value[t * ch : (t + 1) * ch]
            out[t, :, lane:] = tails[t * ch : (t + 1) * ch]
        keep(out, target)
    for made, source, out, target in ((loads[3], adv, out_adv, adv_out), (loads[4], adj, out_adj, adj_out)):
        made.wait()
        out[...] = jnp.swapaxes(source[...].astype(F32), 0, 1).astype(BF)
        keep(out, target.at[0])
    for made in stores:
        made.wait()


def body(state_in, new_state, cot_early, cot_late, kernel_first, kernel_mid, kernel_last):
    steps, lats = lax.axis_size("step"), lax.axis_size("lat")
    ch, rows, width = new_state.shape
    hid = kernel_mid.shape[1]
    taps = kernel_mid.shape[0]
    cp = -(-ch // 16) * 16
    plan = Plan(steps, lats, ch, hid)
    lane = plan.lane
    scale = 1.0 / math.sqrt(2.0 * steps * rows * lats * width)

    vmem = pl.BlockSpec(memory_space=pltpu.VMEM)
    shape = jax.ShapeDtypeStruct
    ext, ext_1, ext_2 = rows + 14, rows + 12, rows + 8
    band_in = ((ch, rows, width), BF)
    moved = [band_in] * 4 + [
        ((taps, ch, hid), BF), ((taps, hid, hid), BF), ((taps, ch, hid), BF),
        ((rows, ch, width), BF), ((rows, ch, width), BF), ((plan.rows, lane), BF),
    ]
    scratch = [((ext, ch, width), BF)] * 5 + [
        ((hid, 9 * cp), BF), ((hid, 9 * hid), BF), ((3 * cp, 3 * hid), BF),
        ((3 * cp, 3 * hid), BF), ((hid, 9 * hid), BF), ((hid, 9 * cp), BF),
        ((ext, 3 * cp, width), BF), ((ext, 3 * cp, width), BF),
        ((ext_1, 3 * hid, width), BF), ((ext_1, 3 * hid, width), BF),
        ((ext_2, hid, width), BF), ((ext_2, hid, width), BF),
        ((ext_1, hid, width), BF), ((ext_1, hid, width), BF),
        ((ext_2, hid, width), BF),
        ((ext, 3 * cp, width), BF), ((rows + 6, 3 * hid, width), BF), ((rows + 2, hid, width), BF),
        ((rows + 6, hid, width), F32),
        ((rows, ch, width), BF), ((rows, ch, width), BF),
        ((3, 3 * cp, hid), F32), ((3, 3, hid, hid), F32), ((3, 3 * cp, hid), F32),
        ((plan.rows, lane), BF),
    ]
    for dims in plan.shapes:
        scratch += [(d + (lane,), BF) for d in dims]
    sems = pltpu.SemaphoreType.DMA
    band_shape = shape((rows, ch, width), BF)
    anywhere = pl.BlockSpec(memory_space=pl.ANY)
    advanced, adjoint, packed = pl.pallas_call(
        functools.partial(mega_kernel, rows, width, steps, lats, scale, plan),
        out_shape=[band_shape, band_shape, shape((plan.rows, lane), BF)],
        in_specs=[anywhere] * 7,
        out_specs=[anywhere] * 3,
        scratch_shapes=[pltpu.VMEM(*s) for s in moved] + [
            sems((7,)), sems((2 + len(plan.segments),)),
        ] + [pltpu.VMEM(*s) for s in scratch] + [sems((16,)), sems((16,)), sems((plan.slots,)), sems((plan.slots,))],
        compiler_params=pltpu.CompilerParams(
            collective_id=0, has_side_effects=True, vmem_limit_bytes=60 * 1024 * 1024
        ),
        name="rollout",
    )(state_in, new_state, cot_late, cot_early, kernel_first, kernel_mid, kernel_last)
    return pl.pallas_call(
        functools.partial(unpack_kernel, plan),
        out_shape=[
            shape((1, ch, rows, width), BF), shape((1, ch, rows, width), BF),
            shape((taps, ch, hid), F32), shape((taps, hid, hid), F32), shape((taps, ch, hid), F32),
        ],
        in_specs=[anywhere] * 3,
        out_specs=[anywhere] * 5,
        scratch_shapes=[
            pltpu.VMEM(*s) for s in moved[7:] + [band_in, band_in] + [
                ((taps, ch, hid), F32), ((taps, hid, hid), F32), ((taps, ch, hid), F32),
            ]
        ] + [sems((5,)), sems((7,))],
        compiler_params=pltpu.CompilerParams(vmem_limit_bytes=60 * 1024 * 1024),
        name="unpack_terms",
    )(advanced, adjoint, packed)


def solution(mesh):
    banded = P("step", None, "lat", None)
    return jax.shard_map(
        body,
        mesh=mesh,
        in_specs=(banded, P(None, "lat", None), banded, banded, P(), P(), P()),
        out_specs=(banded, banded, P(), P(), P()),
        check_vma=False,
    )
```

```python
import functools
import math

import jax
import jax.numpy as jnp
from jax import lax
from jax.experimental import pallas as pl
from jax.experimental.pallas import tpu as pltpu
from jax.sharding import PartitionSpec as P

MESH = pl.DeviceIdType.MESH
BF = jnp.bfloat16
F32 = jnp.float32
HALO = 7
NT = (((1,), (1,)), ((), ()))


def gelu_pair(a):
    c0 = math.sqrt(2.0 / math.pi)
    c1 = c0 * 0.044715
    sq = a * a
    t = jnp.tanh(a * (c0 + c1 * sq))
    half = 0.5 + 0.5 * t
    slope = half + (a * (1.0 - t * t)) * (0.5 * c0 + (1.5 * c1) * sq)
    return a * half, slope


def row_pair(src, row, offsets):
    return jnp.concatenate(
        [jnp.concatenate([src[row + k + o] for o in offsets], axis=0) for k in range(2)], axis=1
    )


def shifted(value, shift):
    width = value.shape[1]
    if shift == 0:
        return value
    column = lax.broadcasted_iota(jnp.int32, value.shape, 1)
    moved = pltpu.roll(value, (-shift) % width, 1)
    good = (column < width - shift) if shift > 0 else (column >= -shift)
    return jnp.where(good, moved, 0.0)


def put_spread(dst, row, value, dilation, sign):
    channels, pitch = value.shape[0], dst.shape[1] // 3
    for j in range(3):
        dst[row, j * pitch : j * pitch + channels, :] = shifted(value, sign * dilation * (j - 1)).astype(BF)


def gathered(total, dilation, sign):
    channels = total.shape[0] // 3
    acc = total[channels : 2 * channels]
    for j in (0, 2):
        acc = acc + shifted(total[j * channels : (j + 1) * channels], sign * dilation * (j - 1))
    return acc


def each(count, work, unroll=None):
    pl.loop(0, count, unroll=count if unroll is None else unroll)(work)


def dot(a, b):
    return jnp.dot(a, b, preferred_element_type=F32)


def nt(a, b):
    return lax.dot_general(a, b, NT, preferred_element_type=F32)


def side(src, row, count, low, high):
    return jnp.concatenate([src[row + k, low:high] for k in range(count)], axis=1)


def tall(kernel, spare):
    taps, _, hid = kernel.shape
    block = [kernel[t].astype(F32) for t in range(taps)]
    if spare:
        block = [jnp.concatenate([b, jnp.zeros((spare, hid), F32)], axis=0) for b in block]
    return block


def lay_out_across(kernel, out, spare):
    out[...] = jnp.transpose(jnp.concatenate(tall(kernel, spare), axis=0)).astype(BF)


def lay_out_along(kernel, out):
    out[...] = jnp.concatenate(tall(kernel, 0), axis=1).astype(BF)


def lay_out_stacked(kernel, out, spare):
    blocks = tall(kernel, spare)
    size = blocks[0].shape[0]
    for j in range(3):
        out[j * size : (j + 1) * size, :] = jnp.concatenate(
            [blocks[3 * i + j] for i in range(3)], axis=1
        ).astype(BF)


def pack_terms(blocks, lane, size):
    rest = blocks[0].shape[1] - lane
    main = jnp.concatenate([b[:, :lane] for b in blocks], axis=0)
    tails = jnp.concatenate([b[:, lane:] for b in blocks], axis=0)
    count = main.shape[0]
    cut = half_rows(count)
    low = tails[cut:]
    if cut * 2 > count:
        low = jnp.concatenate([low, jnp.zeros((2 * cut - count, rest), F32)], axis=0)
    parts = [main, jnp.concatenate([tails[:cut], low], axis=1)]
    if size > count + cut:
        parts.append(jnp.zeros((size - count - cut, lane), F32))
    return jnp.concatenate(parts, axis=0).astype(BF)


def half_rows(count):
    return -(-count // 16) * 8


class Plan:
    def __init__(self, steps, lats, ch, hid):
        devices = steps * lats
        unit = 16 * devices
        self.lane = 128
        taps = 9
        small = taps * ch + half_rows(taps * ch)
        self.mid_tap = hid + hid // 2
        mid = taps * self.mid_tap
        self.small = -(-small // 16) * 16
        self.mid, self.last = 0, mid
        units = -(-(mid + self.small) // unit)
        sizes = [2, 2, units - 4] if units >= 5 else [1, units - 1] if units >= 2 else [units]
        edge = 0
        self.segments, self.taps_ready = [], []
        for size in sizes:
            self.segments.append((edge, 16 * size))
            edge += size * unit
            self.taps_ready.append(min(taps, -(-edge // self.mid_tap)))
        self.taps_ready[-1] = taps
        self.first = edge
        first_units = -(-self.small // unit)
        self.segments.append((edge, 16 * first_units))
        self.gap = (self.last + self.small, self.first)
        self.rows = edge + first_units * unit
        chips = devices // 2
        pairs = steps // 2
        self.shapes, self.slots = [], 0
        for _, piece in self.segments:
            half, wedge = chips * piece, lats * piece
            self.shapes.append([
                (half,), (half,), (max(pairs - 1, 1), wedge), (wedge,), (max(lats - 1, 1), piece),
            ])
            self.slots += 2 + 2 * (pairs - 1) + 2 * (lats - 1)


def mega_kernel(
    rows, width, steps, lats, scale, plan,
    state_in, new_in, late_in, early_in, kf_in, km_in, kl_in,
    adv_out, adj_out, packed,
    state, new, late, early, kf, km, kl, adv, adj, full, load, store,
    xs, xl, cl, ce, got, w1, w2, w3o, w1o, w2b, w3b,
    v3e, v3l, h1e, h1l, h2e, h2l, s1e, s1l, s2e, c3, g2s, g1, b2, out_e, adj_l,
    tf, tm, tl, src, *rest,
):
    buffers = []
    for dims in plan.shapes:
        buffers.append(rest[: len(dims)])
        rest = rest[len(dims) :]
    send, recv, send_r, recv_r = rest
    lat = lax.axis_index("lat")
    step = lax.axis_index("step")
    ch = xs.shape[1]
    cp, hid = c3.shape[1] // 3, w2.shape[0]
    spare = cp - ch
    ext = rows + 2 * HALO
    pairs = steps // 2
    core = lax.rem(step, 2)
    pair = step // 2
    has_low, has_high = lat > 0, lat < lats - 1
    first_step = step == 0

    def present(s, l):
        return (s >= 0) & (s < steps) & (l >= 0) & (l < lats)

    partner = {"step": pair * 2 + (1 - core)}

    def pair_peer(k):
        return {"step": lax.rem(pair + k, pairs) * 2 + core}

    def lat_peer(k):
        return {"lat": lax.rem(lat + k, lats)}

    loads = {}
    for n, (name, source, target) in enumerate((
        ("state", state_in.at[0], state), ("kf", kf_in, kf), ("new", new_in, new), ("km", km_in, km),
        ("late", late_in.at[0], late), ("early", early_in.at[0], early), ("kl", kl_in, kl),
    )):
        loads[name] = pltpu.make_async_copy(source, target, load.at[n])
        loads[name].start()
    stores = []

    def keep(source, target):
        made = pltpu.make_async_copy(source, target, store.at[len(stores)])
        made.start()
        stores.append(made)

    barrier = pltpu.get_barrier_semaphore()
    always = [partner] + [pair_peer(k) for k in range(1, pairs)] + [lat_peer(k) for k in range(1, lats)]
    total = jnp.int32(len(always))
    for peer in always:
        pl.semaphore_signal(barrier, inc=1, device_id=peer, device_id_type=MESH)
    for s in (step - 1, step + 1):
        for l in (lat - 1, lat, lat + 1):
            there = present(s, l)

            @pl.when(there)
            def _(s=s, l=l):
                pl.semaphore_signal(barrier, inc=1, device_id={"step": s, "lat": l}, device_id_type=MESH)

            total = total + there.astype(jnp.int32)

    def place(wide, block):
        wide[HALO : HALO + rows] = jnp.swapaxes(block.astype(F32), 0, 1).astype(BF)

    def blank_edges(wide):
        @pl.when(jnp.logical_not(has_low))
        def _():
            wide[:HALO] = jnp.zeros((HALO, ch, width), BF)

        @pl.when(jnp.logical_not(has_high))
        def _():
            wide[HALO + rows :] = jnp.zeros((HALO, ch, width), BF)

    def remote(source, target, k, peer):
        return pltpu.make_async_remote_copy(
            src_ref=source, dst_ref=target, send_sem=send.at[k], recv_sem=recv.at[k],
            device_id=peer, device_id_type=MESH,
        )

    def halo(wide, k):
        up = remote(wide.at[pl.ds(rows, HALO)], wide.at[pl.ds(0, HALO)], k, {"lat": lat + 1})
        down = remote(wide.at[pl.ds(HALO, HALO)], wide.at[pl.ds(HALO + rows, HALO)], k + 1, {"lat": lat - 1})
        return up, down

    def start_halo(both, extra=None):
        up, down = both
        pl.when(has_high if extra is None else has_high & extra)(up.start)
        pl.when(has_low if extra is None else has_low & extra)(down.start)

    def wait_halo(both, extra=None):
        up, down = both
        low = has_low if extra is None else has_low & extra
        high = has_high if extra is None else has_high & extra
        pl.when(low)(up.wait_recv)
        pl.when(high)(down.wait_recv)
        pl.when(high)(up.wait_send)
        pl.when(low)(down.wait_send)

    def kept(value, row):
        g = lat * rows + (row - HALO)
        return jnp.where((g >= 0) & (g < rows * lats), value, 0.0)

    def halves(total):
        return total[:, :width], total[:, width:]

    def spread_rows(wide, dst, first, count, dilation, sign):
        each(count, lambda r: put_spread(dst, first + r, wide[first + r].astype(F32), dilation, sign))

    def conv1(v3, s1, h1, row):
        for k, part in enumerate(halves(dot(w1[...], row_pair(v3, row, (0, 1, 2))))):
            value, slope = gelu_pair(part)
            s1[row + k] = slope.astype(BF)
            put_spread(h1, row + k, kept(value, row + k + 1), 2, 1)

    def conv2(h1, h2, row):
        result = []
        for k, part in enumerate(halves(dot(w2[...], row_pair(h1, row, (0, 2, 4))))):
            value, slope = gelu_pair(part)
            h2[row + k] = kept(value, row + k + 3).astype(BF)
            result.append(slope)
        return result

    def conv3(x, h2, out, row):
        for k, part in enumerate(halves(dot(w3o[...], row_pair(h2, row, (0, 4, 8))))):
            out[row + k] = (x[row + k + HALO].astype(F32) + gathered(part, 4, 1)[:ch]).astype(BF)

    def back1(s1, row):
        for k, part in enumerate(halves(dot(w2b[...], row_pair(g2s, row, (4, 2, 0))))):
            delta = s1[row + k + 5].astype(F32) * part
            g1[row + k] = kept(delta, row + k + 6).astype(BF)

    def back0(cot, out, row):
        for k, part in enumerate(halves(dot(w1o[...], row_pair(g1, row, (2, 1, 0))))):
            out[row + k] = (cot[row + k + HALO].astype(F32) + gathered(part, 1, -1)[:ch]).astype(BF)

    def put_g2(row, delta):
        put_spread(g2s, row, kept(delta, row + 4), 2, -1)

    def last_term(h2, i):
        return nt(side(c3, 3 + (2 - i) * 4, rows, 0, 3 * cp), side(h2, 4, rows, 0, hid))

    def first_term(v3, i):
        return nt(side(v3, 6 + i, rows, 0, 3 * cp), side(g1, 1, rows, 0, hid))

    def mid_term(h1, i, j):
        return nt(side(h1, 6, rows, hid, 2 * hid), side(g2s, 1 + (2 - i) * 2, rows, j * hid, (j + 1) * hid))

    half_band = rows // 2

    def step_moves(block, target, distance, k):
        groups = []
        for group in (
            ((0, 0, half_band, HALO), (-1, 0, HALO, HALO + rows)),
            ((0, half_band, rows - half_band, HALO + half_band), (1, rows - HALO, HALO, 0)),
        ):
            moves = []
            for shift, source, count, into in group:
                made = remote(
                    block.at[pl.ds(source, count)], target.at[pl.ds(into, count)], k,
                    {"step": step + distance, "lat": lat + shift},
                )
                k += 1
                moves.append((present(step + distance, lat + shift), present(step - distance, lat - shift), into, count, made))
            groups.append(moves)
        return groups

    def start_moves(moves):
        for goes, comes, into, size, made in moves:
            pl.when(goes)(made.start)

    halo_state, halo_new, halo_late, halo_early = halo(xs, 0), halo(xl, 2), halo(cl, 4), halo(ce, 6)
    state_low, state_high = step_moves(out_e, xl, 1, 8)
    cot_low, cot_high = step_moves(adj_l, got, -1, 12)

    loads["state"].wait()
    place(xs, state[...])
    blank_edges(xs)
    pl.semaphore_wait(barrier, total)
    start_halo(halo_state)
    loads["new"].wait()
    pl.when(first_step)(lambda: place(xl, new[...]))
    start_halo(halo_new, first_step)
    blank_edges(xl)
    for wide in (v3e, v3l, c3):
        for j in range(3):
            wide[:, j * cp + ch : (j + 1) * cp, :] = jnp.zeros((ext, spare, width), BF)
    loads["kf"].wait()
    lay_out_across(kf, w1, spare)
    spread_rows(xs, v3e, HALO, rows, 1, 1)
    inner_first = HALO + 1
    inner_pairs = (rows - 4) // 2
    low_pairs = inner_first // 2
    high_first = inner_first + 2 * inner_pairs
    high_pairs = (rows + 12 - high_first) // 2
    half_pairs = half_band // 2
    each(inner_pairs, lambda c: conv1(v3e, s1e, h1e, inner_first + 2 * c))
    loads["km"].wait()
    lay_out_across(km, w2, 0)

    def early_conv2(row):
        for k, slope in enumerate(conv2(h1e, h2e, row)):
            s2e[row + k] = slope.astype(BF)

    each(inner_pairs - 2, lambda c: early_conv2(inner_first + 2 * c))
    loads["late"].wait()
    place(cl, late[...])
    blank_edges(cl)
    loads["early"].wait()
    place(ce, early[...])
    blank_edges(ce)
    loads["kl"].wait()
    lay_out_stacked(kl, w3o, spare)
    wait_halo(halo_state)
    start_halo(halo_late)
    spread_rows(xs, v3e, 0, HALO, 1, 1)
    each(low_pairs, lambda c: conv1(v3e, s1e, h1e, 2 * c))
    each(low_pairs, lambda c: early_conv2(2 * c))
    each(half_pairs, lambda c: conv3(xs, h2e, out_e, 2 * c))
    start_moves(state_low)
    spread_rows(xs, v3e, HALO + rows, HALO, 1, 1)
    each(high_pairs, lambda c: conv1(v3e, s1e, h1e, high_first + 2 * c))
    each(high_pairs, lambda c: early_conv2(high_first - 4 + 2 * c))
    each(half_pairs, lambda c: conv3(xs, h2e, out_e, half_band + 2 * c))
    start_moves(state_high)
    start_halo(halo_early)

    lay_out_across(kl, w3b, spare)
    lay_out_along(km, w2b)
    lay_out_stacked(kf, w1o, spare)
    wait_halo(halo_late)
    spread_rows(cl, c3, 0, ext, 4, -1)

    def late_back2(c):
        for k, part in enumerate(halves(dot(w3b[...], row_pair(c3, 2 * c, (8, 4, 0))))):
            b2[2 * c + k] = part

    each((rows + 6) // 2, late_back2)
    def late_conv2(row):
        for k, slope in enumerate(conv2(h1l, h2l, row)):
            r = row + k - 1
            put_g2(r, slope * b2[r])

    state_moves, cot_moves = state_low + state_high, cot_low + cot_high
    for goes, comes, into, size, made in (state_moves[0], state_moves[2]):
        pl.when(comes)(made.wait_recv)
    spread_rows(xl, v3l, HALO, rows, 1, 1)
    each(inner_pairs, lambda c: conv1(v3l, s1l, h1l, inner_first + 2 * c))
    each(inner_pairs - 2, lambda c: late_conv2(inner_first + 2 * c))
    wait_halo(halo_new, first_step)
    for goes, comes, into, size, made in state_moves[1:2]:
        pl.when(comes)(made.wait_recv)
    spread_rows(xl, v3l, HALO + rows, HALO, 1, 1)
    each(high_pairs, lambda c: conv1(v3l, s1l, h1l, high_first + 2 * c))
    each(high_pairs - 1, lambda c: late_conv2(high_first - 4 + 2 * c))
    conv2_last = conv2(h1l, h2l, rows + 6)
    put_g2(rows + 5, conv2_last[0] * b2[rows + 5])
    each(half_pairs + 1, lambda c: back1(s1l, half_band + 2 * c))
    each(half_pairs, lambda c: back0(cl, adj_l, half_band + 2 * c))
    start_moves(cot_high)
    for goes, comes, into, size, made in state_moves[3:]:
        pl.when(comes)(made.wait_recv)
    spread_rows(xl, v3l, 0, HALO, 1, 1)
    each(low_pairs, lambda c: conv1(v3l, s1l, h1l, 2 * c))
    conv2_first = conv2(h1l, h2l, 0)
    put_g2(0, conv2_first[1] * b2[0])
    each(low_pairs - 1, lambda c: late_conv2(2 * c + 2))
    each(half_pairs, lambda c: back1(s1l, 2 * c))
    each(half_pairs, lambda c: back0(cl, adj_l, 2 * c))
    start_moves(cot_low)

    @pl.loop(0, 3)
    def _(i):
        tl[i] = last_term(h2l, i)
        for j in range(3):
            tm[i, j] = mid_term(h1l, i, j)
        tf[i] = first_term(v3l, i)

    wait_halo(halo_early)
    def add_cot(moves):
        for goes, comes, into, size, made in moves:
            @pl.when(comes)
            def _(into=into, size=size, made=made):
                made.wait_recv()
                for r in range(into, into + size):
                    ce[r] = (ce[r].astype(F32) + got[r].astype(F32)).astype(BF)

    add_cot((cot_moves[0], cot_moves[2]))
    spread_rows(ce, c3, HALO, rows, 4, -1)
    add_cot((cot_moves[1], cot_moves[3]))
    spread_rows(ce, c3, 0, HALO, 4, -1)
    spread_rows(ce, c3, HALO + rows, HALO, 4, -1)

    slots = [0]

    def rows_at(start, size):
        return pl.ds(pl.multiple_of(start, 16), size)

    def copy(source, target, peer):
        slot = slots[0]
        slots[0] += 1
        made = pltpu.make_async_remote_copy(
            src_ref=source, dst_ref=target, send_sem=send_r.at[slot], recv_sem=recv_r.at[slot],
            device_id=peer, device_id_type=MESH,
        )
        made.start()
        return made

    def keep_segment(base, piece):
        whole = pl.ds(base, 2 * pairs * lats * piece)
        keep(full.at[whole], packed.at[whole])

    def summing(q):
        base, piece = plan.segments[q]
        got_a, part_b, got_b, part_c, got_c = buffers[q]
        half, wedge = pairs * lats * piece, lats * piece
        mine_half = base + core * half
        flying = [copy(src.at[rows_at(base + (1 - core) * half, half)], got_a, partner)]

        def finish():
            for made in flying:
                made.wait()

        yield
        finish()
        part_b[...] = (src[rows_at(mine_half, half), :].astype(F32) + got_a[...].astype(F32)).astype(BF)
        flying = [
            copy(part_b.at[rows_at(lax.rem(pair + k, pairs) * wedge, wedge)], got_b.at[k - 1], pair_peer(k))
            for k in range(1, pairs)
        ]
        yield
        finish()
        total = src[rows_at(mine_half + pair * wedge, wedge), :].astype(F32)
        total = total + got_a[rows_at(pair * wedge, wedge), :].astype(F32)
        for k in range(pairs - 1):
            total = total + got_b[k].astype(F32)
        part_c[...] = total.astype(BF)
        flying = [
            copy(part_c.at[rows_at(lax.rem(lat + k, lats) * piece, piece)], got_c.at[k - 1], lat_peer(k))
            for k in range(1, lats)
        ]
        yield
        finish()
        total = part_c[rows_at(lat * piece, piece), :].astype(F32)
        for k in range(lats - 1):
            total = total + got_c[k].astype(F32)
        mine = rows_at(mine_half + pair * wedge + lat * piece, piece)
        full[mine, :] = (total * scale).astype(BF)
        flying = [copy(full.at[mine], full.at[mine], lat_peer(k)) for k in range(1, lats)]
        yield
        finish()
        held = full.at[rows_at(mine_half + pair * wedge, wedge)]
        flying = [copy(held, held, pair_peer(k)) for k in range(1, pairs)]
        yield
        finish()
        held = full.at[rows_at(mine_half, half)]
        flying = [copy(held, held, partner)]
        yield
        finish()
        keep_segment(base, piece)
        yield

    def blocks_of(terms):
        return [terms[i, j * cp : j * cp + ch] for i in range(3) for j in range(3)]

    lane = plan.lane

    sums = [summing(q) for q in range(len(plan.segments))]
    early_sums, sum_last, sum_first = sums[:-2], sums[-2], sums[-1]

    def advance(*which):
        for one in which:
            next(one, None)

    def early_back2(c):
        for k, part in enumerate(halves(dot(w3b[...], row_pair(c3, 2 * c, (8, 4, 0))))):
            row = 2 * c + k
            put_g2(row, s2e[row + 1].astype(F32) * part)

    each((rows + 6) // 2, early_back2)
    tap = 0
    for k, ready in enumerate(plan.taps_ready):
        for t in range(tap, ready):
            value = tm[t // 3, t % 3] + mid_term(h1e, t // 3, t % 3)
            start = plan.mid + t * plan.mid_tap
            src[start : start + plan.mid_tap, :] = pack_terms([value], lane, plan.mid_tap)
        tap = ready
        if k < len(early_sums):
            advance(*early_sums[: k + 1][::-1])

    @pl.loop(0, 3, unroll=3)
    def _(i):
        tl[i] = tl[i] + last_term(h2e, i)

    src[plan.last : plan.last + plan.small, :] = pack_terms(blocks_of(tl), lane, plan.small)
    if plan.gap[1] > plan.gap[0]:
        src[plan.gap[0] : plan.gap[1], :] = jnp.zeros((plan.gap[1] - plan.gap[0], lane), BF)
    advance(sum_last, *early_sums[1:])
    each((rows + 2) // 2, lambda c: back1(s1e, 2 * c))
    advance(sum_last)

    @pl.loop(0, 3, unroll=3)
    def _(i):
        tf[i] = tf[i] + first_term(v3e, i)

    src[plan.first :, :] = pack_terms(blocks_of(tf), lane, plan.rows - plan.first)
    advance(sum_first, *early_sums[:1])
    each(rows // 2, lambda c: back0(ce, adj, 2 * c))
    keep(adj, adj_out)
    advance(sum_first, *early_sums[1:])
    each(rows // 2, lambda c: conv3(xl, h2l, adv, 2 * c))
    keep(adv, adv_out)
    for _ in range(7):
        advance(sum_last, *early_sums[:1], sum_first, *early_sums[1:])

    for goes, comes, into, size, made in state_moves + cot_moves:
        pl.when(goes)(made.wait_send)
    for made in stores:
        made.wait()


def unpack_kernel(
    plan, adv_in, adj_in, packed_in, adv_out, adj_out, first_out, mid_out, last_out,
    adv, adj, packed, out_adv, out_adj, out_first, out_mid, out_last, load, store,
):
    taps, ch, hid = out_first.shape
    lane = plan.lane
    rest = hid - lane
    small = pl.ds(plan.last, plan.small)
    mids = [pl.ds(plan.mid + 3 * group * plan.mid_tap, 3 * plan.mid_tap) for group in range(3)]
    firsts = pl.ds(plan.first, plan.small)
    loads = [
        pltpu.make_async_copy(source, target, load.at[n])
        for n, (source, target) in enumerate((
            *((packed_in.at[part], packed.at[part]) for part in mids),
            (packed_in.at[small], packed.at[small]), (packed_in.at[firsts], packed.at[firsts]),
            (adv_in, adv), (adj_in, adj),
        ))
    ]
    for made in loads:
        made.start()
    stores = []

    def keep(source, target):
        made = pltpu.make_async_copy(source, target, store.at[len(stores)])
        made.start()
        stores.append(made)

    cut = half_rows(hid)
    for group in range(3):
        loads[group].wait()
        for t in range(3 * group, 3 * group + 3):
            start = plan.mid + t * plan.mid_tap
            value = packed[start : start + plan.mid_tap, :].astype(F32)
            out_mid[t, :, :lane] = value[:hid]
            out_mid[t, :cut, lane:] = value[hid : hid + cut, :rest]
            out_mid[t, cut:, lane:] = value[hid : hid + cut, rest:]
        part = pl.ds(3 * group, 3)
        keep(out_mid.at[part], mid_out.at[part])
    for made, start, out, target in (
        (loads[3], plan.last, out_last, last_out), (loads[4], plan.first, out_first, first_out)
    ):
        made.wait()
        count = taps * ch
        cut = half_rows(count)
        value = packed[start : start + plan.small, :].astype(F32)
        tails = value[count : count + cut]
        tails = jnp.concatenate([tails[:, :rest], tails[:, rest:]], axis=0)
        for t in range(taps):
            out[t, :, :lane] = value[t * ch : (t + 1) * ch]
            out[t, :, lane:] = tails[t * ch : (t + 1) * ch]
        keep(out, target)
    for made, source, out, target in ((loads[5], adv, out_adv, adv_out), (loads[6], adj, out_adj, adj_out)):
        made.wait()
        out[...] = jnp.swapaxes(source[...].astype(F32), 0, 1).astype(BF)
        keep(out, target.at[0])
    for made in stores:
        made.wait()


def body(state_in, new_state, cot_early, cot_late, kernel_first, kernel_mid, kernel_last):
    steps, lats = lax.axis_size("step"), lax.axis_size("lat")
    ch, rows, width = new_state.shape
    hid = kernel_mid.shape[1]
    taps = kernel_mid.shape[0]
    cp = -(-ch // 16) * 16
    plan = Plan(steps, lats, ch, hid)
    lane = plan.lane
    scale = 1.0 / math.sqrt(2.0 * steps * rows * lats * width)

    vmem = pl.BlockSpec(memory_space=pltpu.VMEM)
    shape = jax.ShapeDtypeStruct
    ext, ext_1, ext_2 = rows + 14, rows + 12, rows + 8
    band_in = ((ch, rows, width), BF)
    moved = [band_in] * 4 + [
        ((taps, ch, hid), BF), ((taps, hid, hid), BF), ((taps, ch, hid), BF),
        ((rows, ch, width), BF), ((rows, ch, width), BF), ((plan.rows, lane), BF),
    ]
    scratch = [((ext, ch, width), BF)] * 5 + [
        ((hid, 9 * cp), BF), ((hid, 9 * hid), BF), ((3 * cp, 3 * hid), BF),
        ((3 * cp, 3 * hid), BF), ((hid, 9 * hid), BF), ((hid, 9 * cp), BF),
        ((ext, 3 * cp, width), BF), ((ext, 3 * cp, width), BF),
        ((ext_1, 3 * hid, width), BF), ((ext_1, 3 * hid, width), BF),
        ((ext_2, hid, width), BF), ((ext_2, hid, width), BF),
        ((ext_1, hid, width), BF), ((ext_1, hid, width), BF),
        ((ext_2, hid, width), BF),
        ((ext, 3 * cp, width), BF), ((rows + 6, 3 * hid, width), BF), ((rows + 2, hid, width), BF),
        ((rows + 6, hid, width), F32),
        ((rows, ch, width), BF), ((rows, ch, width), BF),
        ((3, 3 * cp, hid), F32), ((3, 3, hid, hid), F32), ((3, 3 * cp, hid), F32),
        ((plan.rows, lane), BF),
    ]
    for dims in plan.shapes:
        scratch += [(d + (lane,), BF) for d in dims]
    sems = pltpu.SemaphoreType.DMA
    band_shape = shape((rows, ch, width), BF)
    anywhere = pl.BlockSpec(memory_space=pl.ANY)
    advanced, adjoint, packed = pl.pallas_call(
        functools.partial(mega_kernel, rows, width, steps, lats, scale, plan),
        out_shape=[band_shape, band_shape, shape((plan.rows, lane), BF)],
        in_specs=[anywhere] * 7,
        out_specs=[anywhere] * 3,
        scratch_shapes=[pltpu.VMEM(*s) for s in moved] + [
            sems((7,)), sems((2 + len(plan.segments),)),
        ] + [pltpu.VMEM(*s) for s in scratch] + [sems((16,)), sems((16,)), sems((plan.slots,)), sems((plan.slots,))],
        compiler_params=pltpu.CompilerParams(
            collective_id=0, has_side_effects=True, vmem_limit_bytes=60 * 1024 * 1024
        ),
        name="rollout",
    )(state_in, new_state, cot_late, cot_early, kernel_first, kernel_mid, kernel_last)
    return pl.pallas_call(
        functools.partial(unpack_kernel, plan),
        out_shape=[
            shape((1, ch, rows, width), BF), shape((1, ch, rows, width), BF),
            shape((taps, ch, hid), F32), shape((taps, hid, hid), F32), shape((taps, ch, hid), F32),
        ],
        in_specs=[anywhere] * 3,
        out_specs=[anywhere] * 5,
        scratch_shapes=[
            pltpu.VMEM(*s) for s in moved[7:] + [band_in, band_in] + [
                ((taps, ch, hid), F32), ((taps, hid, hid), F32), ((taps, ch, hid), F32),
            ]
        ] + [sems((7,)), sems((7,))],
        compiler_params=pltpu.CompilerParams(vmem_limit_bytes=60 * 1024 * 1024),
        name="unpack_terms",
    )(advanced, adjoint, packed)


def solution(mesh):
    banded = P("step", None, "lat", None)
    return jax.shard_map(
        body,
        mesh=mesh,
        in_specs=(banded, P(None, "lat", None), banded, banded, P(), P(), P()),
        out_specs=(banded, banded, P(), P(), P()),
        check_vma=False,
    )
```
